128 devices in a mesh: tm: 32 (over x, y, core), space: 4 (over z).
Axes of the slice: x: 4, y: 4, z: 4, core: 2. Of those that a mesh axis runs over, the one named last changes fastest.
Arguments:
- right_side: float32 [32, 4, 16, 64, 128], P('tm', None, 'space'), may hold values from -4 to 6
- metric: float32 [32, 16, 64, 128], P('tm', 'space'), may hold values from 0.5 to 2
- wall_mask: int32 [16, 64, 128], P('space'), may hold values from 0 to 2, as said below
Outputs:
- solution: float32 [32, 4, 16, 64, 128], P('tm', None, 'space')
The draws below stay inside these ranges and needn't reach their ends.
Inputs may be any that keep to these rules, and one draw needn't show every extreme that they name: `wall_mask`: 0 marks a fluid node, 1 a wall node, 2 an inlet node; inlet nodes lie only in the x-plane 0, and every draw has nodes of all three kinds.
All inputs are finite; a program needn't handle non-finite values.
Results may differ from the reference program's by a relative error of at most 0.0001.
Values sent between devices are 32-bit elements; how exact they have to be, the bound alone decides.
A program may use at most 128 MiB of HBM per device.

```python
import math
import jax
import jax.numpy as jnp
from jax import lax

NY = 64
NZ = 128
CYCLES = 2
NU = 2
COARSE_SWEEPS = 4
TSTEPS = 32
NX = 16


def draw_wall_mask(key, part):
    radius = jax.random.randint(key, (NX,), 40, 61)
    across_y = (2 * jnp.arange(NY, dtype=jnp.int32) + 1 - NY) * 64 // NY
    across_z = (2 * jnp.arange(NZ, dtype=jnp.int32) + 1 - NZ) * 64 // NZ
    reach = across_y[None, :, None] * across_y[None, :, None] + across_z[None, None, :] * across_z[None, None, :]
    outside = reach > radius[:, None, None] * radius[:, None, None]
    planes = jnp.arange(NX, dtype=jnp.int32)
    inlet = jnp.logical_and(planes[:, None, None] == 0, jnp.logical_not(outside))
    return jnp.where(outside, 1, jnp.where(inlet, 2, 0)).astype(jnp.int32)


def draw_right_side(key, part):
    shape = (TSTEPS, 4, NX, NY, NZ)
    noise_key = jax.random.fold_in(key, 7)
    rough = jnp.clip(jax.random.normal(noise_key, shape, jnp.float32), -4.0, 4.0)
    level = 0.8
    steps_at = (jnp.arange(TSTEPS, dtype=jnp.float32) + 0.5) / TSTEPS
    planes_at = (jnp.arange(NX, dtype=jnp.float32) + 0.5) / NX
    weights = jnp.array([1.0, 0.8, 0.6, 0.4], jnp.float32)
    smooth = level + 0.4 * jnp.cos(3.14159265 * steps_at)[:, None, None] * jnp.cos(3.14159265 * planes_at)[None, None, :]
    smooth = smooth * weights[None, :, None]
    return (rough + smooth[:, :, :, None, None]).astype(jnp.float32)


def steps_of(own_key, dims, split, smallest, largest):
    loudness, own = 1.0, jax.random.fold_in(own_key, 6)
    for dim, parts in split:
        draws = jnp.exp(jax.random.uniform(jax.random.fold_in(own, dim), (parts,), jnp.float32, smallest / len(split), largest / len(split)))
        loudness = loudness * jnp.repeat(draws, dims[dim] // parts).reshape([-1 if axis == dim else 1 for axis in range(len(dims))])
    return loudness


def setup_inputs(seed: int = 0) -> dict:
    keys = jax.random.split(jax.random.key(seed), 4)
    return {
        "right_side": draw_right_side(jax.random.fold_in(keys[3], 71), 0),
        "metric": jnp.clip(jnp.exp(math.log(2.0) - 1.3862944 * jax.random.uniform(keys[1], (TSTEPS, NX, NY, NZ), jnp.float32) ** steps_of(keys[1], (TSTEPS, NX, NY, NZ), ((0, 32), (1, 4)), -0.2, 0.2)), 0.5, 2.0),
        "wall_mask": draw_wall_mask(jax.random.fold_in(keys[3], 71), 0),
    }


OMEGA = 0.6


def stencil_apply(padded, metric, earlier, spacing, pinned):
    center = padded[:, :, 1:-1]
    ahead_x = padded[:, :, 2:]
    behind_x = padded[:, :, :-2]
    padded_yz = jnp.pad(center, ((0, 0), (0, 0), (0, 0), (1, 1), (1, 1)))
    ahead_y = padded_yz[:, :, :, 2:, 1:-1]
    behind_y = padded_yz[:, :, :, :-2, 1:-1]
    ahead_z = padded_yz[:, :, :, 1:-1, 2:]
    behind_z = padded_yz[:, :, :, 1:-1, :-2]
    inverse_square = 1.0 / (spacing * spacing)
    half_inverse = 0.5 / spacing
    laplace = (6.0 * center - ahead_x - behind_x - ahead_y - behind_y - ahead_z - behind_z) * inverse_square
    grad_x = (ahead_x[:, 3] - behind_x[:, 3]) * half_inverse
    grad_y = (ahead_y[:, 3] - behind_y[:, 3]) * half_inverse
    grad_z = (ahead_z[:, 3] - behind_z[:, 3]) * half_inverse
    divergence = ((ahead_x[:, 0] - behind_x[:, 0]) + (ahead_y[:, 1] - behind_y[:, 1]) + (ahead_z[:, 2] - behind_z[:, 2])) * half_inverse
    coupling = jnp.stack([grad_x, grad_y, grad_z, divergence], axis=1)
    result = 2.0 * metric[:, None] * (center - earlier) + laplace + coupling
    if pinned is None:
        return result
    return jnp.where(pinned > 0, center, result)


def diagonal_of(metric, spacing, pinned):
    diagonal = 2.0 * metric[:, None] + 6.0 / (spacing * spacing)
    if pinned is None:
        return diagonal
    return jnp.where(pinned > 0, 1.0, diagonal)


def build_pinned(wall_mask):
    moving = (wall_mask > 0).astype(jnp.int32)
    walled = (wall_mask == 1).astype(jnp.int32)
    return jnp.stack([moving, walled, walled, jnp.zeros_like(walled)], axis=0)[None]


def restrict(values):
    dims_all = values.shape
    leading = dims_all[:-3]
    depth_x, height_y, width_z = dims_all[-3:]
    blocks = values.reshape(leading + (depth_x // 2, 2, height_y // 2, 2, width_z // 2, 2))
    offset = len(leading)
    return jnp.sum(blocks, axis=(offset + 1, offset + 3, offset + 5)) * 0.125


def prolong(values):
    dims_all = values.shape
    leading = dims_all[:-3]
    depth_x, height_y, width_z = dims_all[-3:]
    spread = jnp.broadcast_to(values.reshape(leading + (depth_x, 1, height_y, 1, width_z, 1)), leading + (depth_x, 2, height_y, 2, width_z, 2))
    return spread.reshape(leading + (2 * depth_x, 2 * height_y, 2 * width_z))


def coarse_solve(source, metric, spacing):
    diagonal = 2.0 * metric[:, None] + 6.0 / (spacing * spacing)

    def advance(earlier, inputs):
        source_now, metric_now, diagonal_now = inputs
        target = source_now + 2.0 * metric_now[None] * earlier
        iterate = jnp.zeros_like(source_now)
        nothing = jnp.zeros_like(source_now)[None]
        for repeat in range(COARSE_SWEEPS):
            padded = jnp.pad(iterate[None], ((0, 0), (0, 0), (1, 1), (0, 0), (0, 0)))
            applied = stencil_apply(padded, metric_now[None], nothing, spacing, None)[0]
            iterate = iterate + (target - applied) / diagonal_now
        return iterate, iterate

    initial = jnp.zeros_like(source[0])
    final_state, history = lax.scan(advance, initial, (source, metric, diagonal))
    return history


def apply_global(values, metric, spacing, pinned):
    padded = jnp.pad(values, ((0, 0), (0, 0), (1, 1), (0, 0), (0, 0)))
    earlier = jnp.concatenate([jnp.zeros_like(values[:1]), values[:-1]], axis=0)
    return stencil_apply(padded, metric, earlier, spacing, pinned)


def reference(right_side, metric, wall_mask):
    pinned = build_pinned(wall_mask)
    metric_one = restrict(metric)
    metric_two = restrict(metric_one)
    metrics = (metric, metric_one)
    pinned_levels = (pinned, None)

    def cycle(depth, values, source):
        spacing = 2.0 ** depth
        diagonal = diagonal_of(metrics[depth], spacing, pinned_levels[depth])
        for repeat in range(NU):
            values = values + OMEGA * (source - apply_global(values, metrics[depth], spacing, pinned_levels[depth])) / diagonal
        residual = source - apply_global(values, metrics[depth], spacing, pinned_levels[depth])
        coarse_source = restrict(residual)
        if depth == 1:
            correction = coarse_solve(coarse_source, metric_two, 4.0)
        else:
            correction = cycle(1, jnp.zeros_like(coarse_source), coarse_source)
        values = values + prolong(correction)
        for repeat in range(NU):
            values = values + OMEGA * (source - apply_global(values, metrics[depth], spacing, pinned_levels[depth])) / diagonal
        return values

    solution = jnp.zeros_like(right_side)
    for repeat in range(CYCLES):
        solution = cycle(0, solution, right_side)
    return solution
```

```python
import jax
import jax.numpy as jnp
from jax import lax
from jax.sharding import PartitionSpec as P

CYCLES = 2
NU = 2
COARSE_SWEEPS = 4


OMEGA = 0.6


def with_halo(block, sides, width):
    for axis, dim in sides:
        count = lax.axis_size(axis)
        forward = [(i, i + 1) for i in range(count - 1)]
        backward = [(target, source) for source, target in forward]
        low = lax.ppermute(
            lax.slice_in_dim(block, block.shape[dim] - width, None, axis=dim), axis, forward
        )
        high = lax.ppermute(lax.slice_in_dim(block, 0, width, axis=dim), axis, backward)
        block = jnp.concatenate([low, block, high], axis=dim)
    return block


def from_behind(array, axis, by):
    size = lax.axis_size(axis)
    pairs = [(i, i + by) for i in range(size) if 0 <= i + by < size]
    return lax.ppermute(array, axis, pairs)


def stencil_apply(padded, metric, earlier, spacing, pinned):
    center = padded[:, :, 1:-1]
    ahead_x = padded[:, :, 2:]
    behind_x = padded[:, :, :-2]
    padded_yz = jnp.pad(center, ((0, 0), (0, 0), (0, 0), (1, 1), (1, 1)))
    ahead_y = padded_yz[:, :, :, 2:, 1:-1]
    behind_y = padded_yz[:, :, :, :-2, 1:-1]
    ahead_z = padded_yz[:, :, :, 1:-1, 2:]
    behind_z = padded_yz[:, :, :, 1:-1, :-2]
    inverse_square = 1.0 / (spacing * spacing)
    half_inverse = 0.5 / spacing
    laplace = (
        6.0 * center - ahead_x - behind_x - ahead_y - behind_y - ahead_z - behind_z
    ) * inverse_square
    grad_x = (ahead_x[:, 3] - behind_x[:, 3]) * half_inverse
    grad_y = (ahead_y[:, 3] - behind_y[:, 3]) * half_inverse
    grad_z = (ahead_z[:, 3] - behind_z[:, 3]) * half_inverse
    divergence = (
        ahead_x[:, 0]
        - behind_x[:, 0]
        + (ahead_y[:, 1] - behind_y[:, 1])
        + (ahead_z[:, 2] - behind_z[:, 2])
    ) * half_inverse
    coupling = jnp.stack([grad_x, grad_y, grad_z, divergence], axis=1)
    result = 2.0 * metric[:, None] * (center - earlier) + laplace + coupling
    if pinned is None:
        return result
    return jnp.where(pinned > 0, center, result)


def diagonal_of(metric, spacing, pinned):
    diagonal = 2.0 * metric[:, None] + 6.0 / (spacing * spacing)
    if pinned is None:
        return diagonal
    return jnp.where(pinned > 0, 1.0, diagonal)


def build_pinned(wall_mask):
    moving = (wall_mask > 0).astype(jnp.int32)
    walled = (wall_mask == 1).astype(jnp.int32)
    return jnp.stack([moving, walled, walled, jnp.zeros_like(walled)], axis=0)[None]


def restrict(values):
    dims_all = values.shape
    leading = dims_all[:-3]
    depth_x, height_y, width_z = dims_all[-3:]
    blocks = values.reshape(leading + (depth_x // 2, 2, height_y // 2, 2, width_z // 2, 2))
    offset = len(leading)
    return jnp.sum(blocks, axis=(offset + 1, offset + 3, offset + 5)) * 0.125


def prolong(values):
    dims_all = values.shape
    leading = dims_all[:-3]
    depth_x, height_y, width_z = dims_all[-3:]
    spread = jnp.broadcast_to(
        values.reshape(leading + (depth_x, 1, height_y, 1, width_z, 1)),
        leading + (depth_x, 2, height_y, 2, width_z, 2),
    )
    return spread.reshape(leading + (2 * depth_x, 2 * height_y, 2 * width_z))


def coarse_solve(source, metric, spacing):
    diagonal = 2.0 * metric[:, None] + 6.0 / (spacing * spacing)

    def advance(earlier, inputs):
        source_now, metric_now, diagonal_now = inputs
        target = source_now + 2.0 * metric_now[None] * earlier
        iterate = jnp.zeros_like(source_now)
        nothing = jnp.zeros_like(source_now)[None]
        for repeat in range(COARSE_SWEEPS):
            padded = jnp.pad(iterate[None], ((0, 0), (0, 0), (1, 1), (0, 0), (0, 0)))
            applied = stencil_apply(padded, metric_now[None], nothing, spacing, None)[0]
            iterate = iterate + (target - applied) / diagonal_now
        return (iterate, iterate)

    initial = jnp.zeros_like(source[0])
    final_state, history = lax.scan(advance, initial, (source, metric, diagonal))
    return history


def apply_local(values, metric, spacing, pinned):
    padded = with_halo(values, (("space", 2),), 1)
    arrived = from_behind(values, "tm", 1)
    earlier = jnp.concatenate([arrived, values[:-1]], axis=0)
    return stencil_apply(padded, metric, earlier, spacing, pinned)


def assemble(flat_source, flat_metric, time_devs, plane_devs, local_dims):
    local_steps, components, planes, height_y, width_z = local_dims
    whole_source = flat_source.reshape(
        time_devs, plane_devs, local_steps, components, planes, height_y, width_z
    )
    whole_source = whole_source.transpose(0, 2, 3, 1, 4, 5, 6).reshape(
        time_devs * local_steps, components, plane_devs * planes, height_y, width_z
    )
    whole_metric = flat_metric.reshape(
        time_devs, plane_devs, local_steps, planes, height_y, width_z
    )
    whole_metric = whole_metric.transpose(0, 2, 1, 3, 4, 5).reshape(
        time_devs * local_steps, plane_devs * planes, height_y, width_z
    )
    return (whole_source, whole_metric)


def coarse_correction(source, metric_two, gathered):
    time_devs = lax.axis_size("tm")
    plane_devs = lax.axis_size("space")
    time_at = lax.axis_index("tm")
    plane_at = lax.axis_index("space")
    local_dims = source.shape
    local_steps, components, planes, height_y, width_z = local_dims
    source_flat = source.reshape(1, -1)
    cut = source_flat.shape[1]
    if "metric" in gathered:
        flat_source = lax.all_gather(source_flat, ("tm", "space"), axis=0, tiled=True)
        flat_metric = gathered["metric"]
    else:
        both = jnp.concatenate([source_flat, metric_two.reshape(1, -1)], axis=1)
        flat_both = lax.all_gather(both, ("tm", "space"), axis=0, tiled=True)
        flat_source = flat_both[:, :cut]
        flat_metric = flat_both[:, cut:]
        gathered["metric"] = flat_metric
    whole_source, whole_metric = assemble(
        flat_source, flat_metric, time_devs, plane_devs, local_dims
    )
    solved = coarse_solve(whole_source, whole_metric, 4.0)
    return lax.dynamic_slice(
        solved,
        (time_at * local_steps, 0, plane_at * planes, 0, 0),
        (local_steps, components, planes, height_y, width_z),
    )


def per_device(right_side, metric, wall_mask):
    pinned = build_pinned(wall_mask)
    metric_one = restrict(metric)
    metric_two = restrict(metric_one)
    metrics = (metric, metric_one)
    pinned_levels = (pinned, None)
    gathered = {}

    def cycle(depth, values, source):
        spacing = 2.0**depth
        diagonal = diagonal_of(metrics[depth], spacing, pinned_levels[depth])
        for repeat in range(NU):
            values = (
                values
                + OMEGA
                * (source - apply_local(values, metrics[depth], spacing, pinned_levels[depth]))
                / diagonal
            )
        residual = source - apply_local(values, metrics[depth], spacing, pinned_levels[depth])
        coarse_source = restrict(residual)
        if depth == 1:
            correction = coarse_correction(coarse_source, metric_two, gathered)
        else:
            correction = cycle(1, jnp.zeros_like(coarse_source), coarse_source)
        values = values + prolong(correction)
        for repeat in range(NU):
            values = (
                values
                + OMEGA
                * (source - apply_local(values, metrics[depth], spacing, pinned_levels[depth]))
                / diagonal
            )
        return values

    solution = jnp.zeros_like(right_side)
    for repeat in range(CYCLES):
        solution = cycle(0, solution, right_side)
    return solution


def solution(mesh):
    placed = (
        P("tm", None, "space", None, None),
        P("tm", "space", None, None),
        P("space", None, None),
    )
    return jax.shard_map(
        per_device,
        mesh=mesh,
        in_specs=placed,
        out_specs=P("tm", None, "space", None, None),
        check_vma=False,
    )
```

```python
import functools

import jax
import jax.numpy as jnp
from jax import lax
from jax.experimental import pallas as pl
from jax.experimental.pallas import tpu as pltpu
from jax.sharding import PartitionSpec as P

CYCLES = 2
NU = 2
COARSE_SWEEPS = 4


OMEGA = 0.6


def with_halo(block, sides, width):
    for axis, dim in sides:
        count = lax.axis_size(axis)
        forward = [(i, i + 1) for i in range(count - 1)]
        backward = [(target, source) for source, target in forward]
        low = lax.ppermute(
            lax.slice_in_dim(block, block.shape[dim] - width, None, axis=dim), axis, forward
        )
        high = lax.ppermute(lax.slice_in_dim(block, 0, width, axis=dim), axis, backward)
        block = jnp.concatenate([low, block, high], axis=dim)
    return block


def from_behind(array, axis, by):
    size = lax.axis_size(axis)
    pairs = [(i, i + by) for i in range(size) if 0 <= i + by < size]
    return lax.ppermute(array, axis, pairs)


def stencil_apply(padded, metric, earlier, spacing, pinned):
    center = padded[:, :, 1:-1]
    ahead_x = padded[:, :, 2:]
    behind_x = padded[:, :, :-2]
    padded_yz = jnp.pad(center, ((0, 0), (0, 0), (0, 0), (1, 1), (1, 1)))
    ahead_y = padded_yz[:, :, :, 2:, 1:-1]
    behind_y = padded_yz[:, :, :, :-2, 1:-1]
    ahead_z = padded_yz[:, :, :, 1:-1, 2:]
    behind_z = padded_yz[:, :, :, 1:-1, :-2]
    inverse_square = 1.0 / (spacing * spacing)
    half_inverse = 0.5 / spacing
    laplace = (
        6.0 * center - ahead_x - behind_x - ahead_y - behind_y - ahead_z - behind_z
    ) * inverse_square
    grad_x = (ahead_x[:, 3] - behind_x[:, 3]) * half_inverse
    grad_y = (ahead_y[:, 3] - behind_y[:, 3]) * half_inverse
    grad_z = (ahead_z[:, 3] - behind_z[:, 3]) * half_inverse
    divergence = (
        ahead_x[:, 0]
        - behind_x[:, 0]
        + (ahead_y[:, 1] - behind_y[:, 1])
        + (ahead_z[:, 2] - behind_z[:, 2])
    ) * half_inverse
    coupling = jnp.stack([grad_x, grad_y, grad_z, divergence], axis=1)
    result = 2.0 * metric[:, None] * (center - earlier) + laplace + coupling
    if pinned is None:
        return result
    return jnp.where(pinned > 0, center, result)


def diagonal_of(metric, spacing, pinned):
    diagonal = 2.0 * metric[:, None] + 6.0 / (spacing * spacing)
    if pinned is None:
        return diagonal
    return jnp.where(pinned > 0, 1.0, diagonal)


def build_pinned(wall_mask):
    moving = (wall_mask > 0).astype(jnp.int32)
    walled = (wall_mask == 1).astype(jnp.int32)
    return jnp.stack([moving, walled, walled, jnp.zeros_like(walled)], axis=0)[None]


def restrict(values):
    dims_all = values.shape
    leading = dims_all[:-3]
    depth_x, height_y, width_z = dims_all[-3:]
    blocks = values.reshape(leading + (depth_x // 2, 2, height_y // 2, 2, width_z // 2, 2))
    offset = len(leading)
    return jnp.sum(blocks, axis=(offset + 1, offset + 3, offset + 5)) * 0.125


def prolong(values):
    dims_all = values.shape
    leading = dims_all[:-3]
    depth_x, height_y, width_z = dims_all[-3:]
    spread = jnp.broadcast_to(
        values.reshape(leading + (depth_x, 1, height_y, 1, width_z, 1)),
        leading + (depth_x, 2, height_y, 2, width_z, 2),
    )
    return spread.reshape(leading + (2 * depth_x, 2 * height_y, 2 * width_z))


def coarse_kernel(src_ref, met_ref, out_ref, *, spacing, depth_x, height_y, width_z):
    steps, rows, lanes = src_ref.shape
    inverse_square = 1.0 / (spacing * spacing)
    half_inverse = 0.5 / spacing
    row = lax.broadcasted_iota(jnp.int32, (rows, lanes), 0)
    lane = lax.broadcasted_iota(jnp.int32, (rows, lanes), 1)
    plane = row % depth_x
    part = row // depth_x
    across_z = lane % width_z
    across_y = lane // width_z
    quarter = rows // 4
    zero = jnp.zeros((rows, lanes), jnp.float32)

    def shifted(v, shift, axis, edge):
        size = v.shape[axis]
        return jnp.where(edge, zero, pltpu.roll(v, shift % size, axis))

    def apply(v, two_g):
        ahead_x = shifted(v, -1, 0, plane == depth_x - 1)
        behind_x = shifted(v, 1, 0, plane == 0)
        ahead_y = shifted(v, -width_z, 1, across_y == height_y - 1)
        behind_y = shifted(v, width_z, 1, across_y == 0)
        ahead_z = shifted(v, -1, 1, across_z == width_z - 1)
        behind_z = shifted(v, 1, 1, across_z == 0)
        laplace = (6.0 * v - ahead_x - behind_x - ahead_y - behind_y - ahead_z - behind_z) * inverse_square
        diff_x = ahead_x - behind_x
        diff_y = ahead_y - behind_y
        diff_z = ahead_z - behind_z
        grad_x = pltpu.roll(diff_x, quarter, 0)
        grad_y = pltpu.roll(diff_y, 2 * quarter, 0)
        grad_z = pltpu.roll(diff_z, 3 * quarter, 0)
        divergence = pltpu.roll(diff_x, 3 * quarter, 0) + pltpu.roll(diff_y, 2 * quarter, 0) + pltpu.roll(diff_z, quarter, 0)
        coupling = jnp.where(part == 0, grad_x, jnp.where(part == 1, grad_y, jnp.where(part == 2, grad_z, divergence))) * half_inverse
        return two_g * v + laplace + coupling

    def advance(t, earlier):
        g = met_ref[t]
        two_g = 2.0 * g
        diagonal = two_g + 6.0 / (spacing * spacing)
        target = src_ref[t] + two_g * earlier
        v = zero
        for repeat in range(COARSE_SWEEPS):
            v = v + (target - apply(v, two_g)) / diagonal
        out_ref[t] = v
        return v

    lax.fori_loop(0, steps, advance, zero)


def coarse_solve(source, metric, spacing):
    steps, components, depth_x, height_y, width_z = source.shape
    rows = components * depth_x
    lanes = height_y * width_z
    flat_source = source.reshape(steps, rows, lanes)
    flat_metric = jnp.tile(metric.reshape(steps, depth_x, lanes), (1, components, 1))
    kernel = functools.partial(coarse_kernel, spacing=spacing, depth_x=depth_x, height_y=height_y, width_z=width_z)
    solved = pl.pallas_call(
        kernel,
        out_shape=jax.ShapeDtypeStruct(flat_source.shape, jnp.float32),
    )(flat_source, flat_metric)
    return solved.reshape(source.shape)


def apply_local(values, metric, spacing, pinned):
    padded = with_halo(values, (("space", 2),), 1)
    arrived = from_behind(values, "tm", 1)
    earlier = jnp.concatenate([arrived, values[:-1]], axis=0)
    return stencil_apply(padded, metric, earlier, spacing, pinned)


def assemble(flat_source, flat_metric, time_devs, plane_devs, local_dims):
    local_steps, components, planes, height_y, width_z = local_dims
    whole_source = flat_source.reshape(
        time_devs, plane_devs, local_steps, components, planes, height_y, width_z
    )
    whole_source = whole_source.transpose(0, 2, 3, 1, 4, 5, 6).reshape(
        time_devs * local_steps, components, plane_devs * planes, height_y, width_z
    )
    whole_metric = flat_metric.reshape(
        time_devs, plane_devs, local_steps, planes, height_y, width_z
    )
    whole_metric = whole_metric.transpose(0, 2, 1, 3, 4, 5).reshape(
        time_devs * local_steps, plane_devs * planes, height_y, width_z
    )
    return (whole_source, whole_metric)


def coarse_correction(source, metric_two, gathered):
    time_devs = lax.axis_size("tm")
    plane_devs = lax.axis_size("space")
    time_at = lax.axis_index("tm")
    plane_at = lax.axis_index("space")
    local_dims = source.shape
    local_steps, components, planes, height_y, width_z = local_dims
    source_flat = source.reshape(1, -1)
    cut = source_flat.shape[1]
    if "metric" in gathered:
        flat_source = lax.all_gather(source_flat, ("tm", "space"), axis=0, tiled=True)
        flat_metric = gathered["metric"]
    else:
        both = jnp.concatenate([source_flat, metric_two.reshape(1, -1)], axis=1)
        flat_both = lax.all_gather(both, ("tm", "space"), axis=0, tiled=True)
        flat_source = flat_both[:, :cut]
        flat_metric = flat_both[:, cut:]
        gathered["metric"] = flat_metric
    whole_source, whole_metric = assemble(
        flat_source, flat_metric, time_devs, plane_devs, local_dims
    )
    solved = coarse_solve(whole_source, whole_metric, 4.0)
    return lax.dynamic_slice(
        solved,
        (time_at * local_steps, 0, plane_at * planes, 0, 0),
        (local_steps, components, planes, height_y, width_z),
    )


def per_device(right_side, metric, wall_mask):
    pinned = build_pinned(wall_mask)
    metric_one = restrict(metric)
    metric_two = restrict(metric_one)
    metrics = (metric, metric_one)
    pinned_levels = (pinned, None)
    gathered = {}

    def cycle(depth, values, source):
        spacing = 2.0**depth
        diagonal = diagonal_of(metrics[depth], spacing, pinned_levels[depth])
        for repeat in range(NU):
            values = (
                values
                + OMEGA
                * (source - apply_local(values, metrics[depth], spacing, pinned_levels[depth]))
                / diagonal
            )
        residual = source - apply_local(values, metrics[depth], spacing, pinned_levels[depth])
        coarse_source = restrict(residual)
        if depth == 1:
            correction = coarse_correction(coarse_source, metric_two, gathered)
        else:
            correction = cycle(1, jnp.zeros_like(coarse_source), coarse_source)
        values = values + prolong(correction)
        for repeat in range(NU):
            values = (
                values
                + OMEGA
                * (source - apply_local(values, metrics[depth], spacing, pinned_levels[depth]))
                / diagonal
            )
        return values

    solution = jnp.zeros_like(right_side)
    for repeat in range(CYCLES):
        solution = cycle(0, solution, right_side)
    return solution


def solution(mesh):
    placed = (
        P("tm", None, "space", None, None),
        P("tm", "space", None, None),
        P("space", None, None),
    )
    return jax.shard_map(
        per_device,
        mesh=mesh,
        in_specs=placed,
        out_specs=P("tm", None, "space", None, None),
        check_vma=False,
    )
```

```python
import functools

import jax
import jax.numpy as jnp
from jax import lax
from jax.experimental import pallas as pl
from jax.experimental.pallas import tpu as pltpu
from jax.sharding import PartitionSpec as P

CYCLES = 2
NU = 2
COARSE_SWEEPS = 4


OMEGA = 0.6


def with_halo(block, sides, width):
    for axis, dim in sides:
        count = lax.axis_size(axis)
        forward = [(i, i + 1) for i in range(count - 1)]
        backward = [(target, source) for source, target in forward]
        low = lax.ppermute(
            lax.slice_in_dim(block, block.shape[dim] - width, None, axis=dim), axis, forward
        )
        high = lax.ppermute(lax.slice_in_dim(block, 0, width, axis=dim), axis, backward)
        block = jnp.concatenate([low, block, high], axis=dim)
    return block


def from_behind(array, axis, by):
    size = lax.axis_size(axis)
    pairs = [(i, i + by) for i in range(size) if 0 <= i + by < size]
    return lax.ppermute(array, axis, pairs)


def stencil_apply(padded, metric, earlier, spacing, pinned):
    center = padded[:, :, 1:-1]
    ahead_x = padded[:, :, 2:]
    behind_x = padded[:, :, :-2]
    padded_yz = jnp.pad(center, ((0, 0), (0, 0), (0, 0), (1, 1), (1, 1)))
    ahead_y = padded_yz[:, :, :, 2:, 1:-1]
    behind_y = padded_yz[:, :, :, :-2, 1:-1]
    ahead_z = padded_yz[:, :, :, 1:-1, 2:]
    behind_z = padded_yz[:, :, :, 1:-1, :-2]
    inverse_square = 1.0 / (spacing * spacing)
    half_inverse = 0.5 / spacing
    laplace = (
        6.0 * center - ahead_x - behind_x - ahead_y - behind_y - ahead_z - behind_z
    ) * inverse_square
    grad_x = (ahead_x[:, 3] - behind_x[:, 3]) * half_inverse
    grad_y = (ahead_y[:, 3] - behind_y[:, 3]) * half_inverse
    grad_z = (ahead_z[:, 3] - behind_z[:, 3]) * half_inverse
    divergence = (
        ahead_x[:, 0]
        - behind_x[:, 0]
        + (ahead_y[:, 1] - behind_y[:, 1])
        + (ahead_z[:, 2] - behind_z[:, 2])
    ) * half_inverse
    coupling = jnp.stack([grad_x, grad_y, grad_z, divergence], axis=1)
    result = 2.0 * metric[:, None] * (center - earlier) + laplace + coupling
    if pinned is None:
        return result
    return jnp.where(pinned > 0, center, result)


def diagonal_of(metric, spacing, pinned):
    diagonal = 2.0 * metric[:, None] + 6.0 / (spacing * spacing)
    if pinned is None:
        return diagonal
    return jnp.where(pinned > 0, 1.0, diagonal)


def build_pinned(wall_mask):
    moving = (wall_mask > 0).astype(jnp.int32)
    walled = (wall_mask == 1).astype(jnp.int32)
    return jnp.stack([moving, walled, walled, jnp.zeros_like(walled)], axis=0)[None]


def restrict(values):
    dims_all = values.shape
    leading = dims_all[:-3]
    depth_x, height_y, width_z = dims_all[-3:]
    blocks = values.reshape(leading + (depth_x // 2, 2, height_y // 2, 2, width_z // 2, 2))
    offset = len(leading)
    return jnp.sum(blocks, axis=(offset + 1, offset + 3, offset + 5)) * 0.125


def prolong(values):
    dims_all = values.shape
    leading = dims_all[:-3]
    depth_x, height_y, width_z = dims_all[-3:]
    spread = jnp.broadcast_to(
        values.reshape(leading + (depth_x, 1, height_y, 1, width_z, 1)),
        leading + (depth_x, 2, height_y, 2, width_z, 2),
    )
    return spread.reshape(leading + (2 * depth_x, 2 * height_y, 2 * width_z))


def coarse_kernel(src_ref, met_ref, out_ref, *, spacing, depth_x, height_y, width_z):
    steps, rows, lanes = src_ref.shape
    inverse_square = 1.0 / (spacing * spacing)
    half_inverse = 0.5 / spacing
    row = lax.broadcasted_iota(jnp.int32, (rows, lanes), 0)
    lane = lax.broadcasted_iota(jnp.int32, (rows, lanes), 1)
    plane = row % depth_x
    part = row // depth_x
    across_z = lane % width_z
    across_y = lane // width_z
    quarter = rows // 4
    zero = jnp.zeros((rows, lanes), jnp.float32)

    def shifted(v, shift, axis, edge):
        size = v.shape[axis]
        return jnp.where(edge, zero, pltpu.roll(v, shift % size, axis))

    def apply(v, two_g):
        ahead_x = shifted(v, -1, 0, plane == depth_x - 1)
        behind_x = shifted(v, 1, 0, plane == 0)
        ahead_y = shifted(v, -width_z, 1, across_y == height_y - 1)
        behind_y = shifted(v, width_z, 1, across_y == 0)
        ahead_z = shifted(v, -1, 1, across_z == width_z - 1)
        behind_z = shifted(v, 1, 1, across_z == 0)
        laplace = (6.0 * v - ahead_x - behind_x - ahead_y - behind_y - ahead_z - behind_z) * inverse_square
        diff_x = ahead_x - behind_x
        diff_y = ahead_y - behind_y
        diff_z = ahead_z - behind_z
        grad_x = pltpu.roll(diff_x, quarter, 0)
        grad_y = pltpu.roll(diff_y, 2 * quarter, 0)
        grad_z = pltpu.roll(diff_z, 3 * quarter, 0)
        divergence = pltpu.roll(diff_x, 3 * quarter, 0) + pltpu.roll(diff_y, 2 * quarter, 0) + pltpu.roll(diff_z, quarter, 0)
        coupling = jnp.where(part == 0, grad_x, jnp.where(part == 1, grad_y, jnp.where(part == 2, grad_z, divergence))) * half_inverse
        return two_g * v + laplace + coupling

    def advance(t, earlier):
        g = met_ref[t]
        two_g = 2.0 * g
        diagonal = two_g + 6.0 / (spacing * spacing)
        target = src_ref[t] + two_g * earlier
        v = zero
        for repeat in range(COARSE_SWEEPS):
            v = v + (target - apply(v, two_g)) / diagonal
        out_ref[t] = v
        return v

    lax.fori_loop(0, steps, advance, zero)


def coarse_solve(source, metric, spacing):
    steps, components, depth_x, height_y, width_z = source.shape
    rows = components * depth_x
    lanes = height_y * width_z
    flat_source = source.reshape(steps, rows, lanes)
    flat_metric = jnp.tile(metric.reshape(steps, depth_x, lanes), (1, components, 1))
    kernel = functools.partial(coarse_kernel, spacing=spacing, depth_x=depth_x, height_y=height_y, width_z=width_z)
    solved = pl.pallas_call(
        kernel,
        out_shape=jax.ShapeDtypeStruct(flat_source.shape, jnp.float32),
    )(flat_source, flat_metric)
    return solved.reshape(source.shape)


def apply_local(values, metric, spacing, pinned):
    padded = with_halo(values, (("space", 2),), 1)
    arrived = from_behind(values, "tm", 1)
    earlier = jnp.concatenate([arrived, values[:-1]], axis=0)
    return stencil_apply(padded, metric, earlier, spacing, pinned)


def assemble(flat_source, flat_metric, time_devs, plane_devs, local_dims):
    local_steps, components, planes, height_y, width_z = local_dims
    whole_source = flat_source.reshape(
        time_devs, plane_devs, local_steps, components, planes, height_y, width_z
    )
    whole_source = whole_source.transpose(0, 2, 3, 1, 4, 5, 6).reshape(
        time_devs * local_steps, components, plane_devs * planes, height_y, width_z
    )
    whole_metric = flat_metric.reshape(
        time_devs, plane_devs, local_steps, planes, height_y, width_z
    )
    whole_metric = whole_metric.transpose(0, 2, 1, 3, 4, 5).reshape(
        time_devs * local_steps, plane_devs * planes, height_y, width_z
    )
    return (whole_source, whole_metric)


def gather_all(flat):
    within = lax.all_gather(flat, "space", axis=0, tiled=True)
    return lax.all_gather(within, "tm", axis=0, tiled=True)


def coarse_correction(source, metric_two, gathered):
    time_devs = lax.axis_size("tm")
    plane_devs = lax.axis_size("space")
    time_at = lax.axis_index("tm")
    plane_at = lax.axis_index("space")
    local_dims = source.shape
    local_steps, components, planes, height_y, width_z = local_dims
    source_flat = source.reshape(1, -1)
    cut = source_flat.shape[1]
    if "metric" in gathered:
        flat_source = gather_all(source_flat)
        flat_metric = gathered["metric"]
    else:
        both = jnp.concatenate([source_flat, metric_two.reshape(1, -1)], axis=1)
        flat_both = gather_all(both)
        flat_source = flat_both[:, :cut]
        flat_metric = flat_both[:, cut:]
        gathered["metric"] = flat_metric
    whole_source, whole_metric = assemble(
        flat_source, flat_metric, time_devs, plane_devs, local_dims
    )
    solved = coarse_solve(whole_source, whole_metric, 4.0)
    return lax.dynamic_slice(
        solved,
        (time_at * local_steps, 0, plane_at * planes, 0, 0),
        (local_steps, components, planes, height_y, width_z),
    )


def per_device(right_side, metric, wall_mask):
    pinned = build_pinned(wall_mask)
    metric_one = restrict(metric)
    metric_two = restrict(metric_one)
    metrics = (metric, metric_one)
    pinned_levels = (pinned, None)
    gathered = {}

    def cycle(depth, values, source):
        spacing = 2.0**depth
        diagonal = diagonal_of(metrics[depth], spacing, pinned_levels[depth])
        for repeat in range(NU):
            values = (
                values
                + OMEGA
                * (source - apply_local(values, metrics[depth], spacing, pinned_levels[depth]))
                / diagonal
            )
        residual = source - apply_local(values, metrics[depth], spacing, pinned_levels[depth])
        coarse_source = restrict(residual)
        if depth == 1:
            correction = coarse_correction(coarse_source, metric_two, gathered)
        else:
            correction = cycle(1, jnp.zeros_like(coarse_source), coarse_source)
        values = values + prolong(correction)
        for repeat in range(NU):
            values = (
                values
                + OMEGA
                * (source - apply_local(values, metrics[depth], spacing, pinned_levels[depth]))
                / diagonal
            )
        return values

    solution = jnp.zeros_like(right_side)
    for repeat in range(CYCLES):
        solution = cycle(0, solution, right_side)
    return solution


def solution(mesh):
    placed = (
        P("tm", None, "space", None, None),
        P("tm", "space", None, None),
        P("space", None, None),
    )
    return jax.shard_map(
        per_device,
        mesh=mesh,
        in_specs=placed,
        out_specs=P("tm", None, "space", None, None),
        check_vma=False,
    )
```

```python
import functools

import jax
import jax.numpy as jnp
from jax import lax
from jax.experimental import pallas as pl
from jax.experimental.pallas import tpu as pltpu
from jax.sharding import PartitionSpec as P

CYCLES = 2
NU = 2
COARSE_SWEEPS = 4


OMEGA = 0.6


def with_halo(block, sides, width):
    for axis, dim in sides:
        count = lax.axis_size(axis)
        forward = [(i, i + 1) for i in range(count - 1)]
        backward = [(target, source) for source, target in forward]
        low = lax.ppermute(
            lax.slice_in_dim(block, block.shape[dim] - width, None, axis=dim), axis, forward
        )
        high = lax.ppermute(lax.slice_in_dim(block, 0, width, axis=dim), axis, backward)
        block = jnp.concatenate([low, block, high], axis=dim)
    return block


def from_behind(array, axis, by):
    size = lax.axis_size(axis)
    pairs = [(i, i + by) for i in range(size) if 0 <= i + by < size]
    return lax.ppermute(array, axis, pairs)


def stencil_apply(padded, metric, earlier, spacing, pinned):
    center = padded[:, :, 1:-1]
    ahead_x = padded[:, :, 2:]
    behind_x = padded[:, :, :-2]
    padded_yz = jnp.pad(center, ((0, 0), (0, 0), (0, 0), (1, 1), (1, 1)))
    ahead_y = padded_yz[:, :, :, 2:, 1:-1]
    behind_y = padded_yz[:, :, :, :-2, 1:-1]
    ahead_z = padded_yz[:, :, :, 1:-1, 2:]
    behind_z = padded_yz[:, :, :, 1:-1, :-2]
    inverse_square = 1.0 / (spacing * spacing)
    half_inverse = 0.5 / spacing
    laplace = (
        6.0 * center - ahead_x - behind_x - ahead_y - behind_y - ahead_z - behind_z
    ) * inverse_square
    grad_x = (ahead_x[:, 3] - behind_x[:, 3]) * half_inverse
    grad_y = (ahead_y[:, 3] - behind_y[:, 3]) * half_inverse
    grad_z = (ahead_z[:, 3] - behind_z[:, 3]) * half_inverse
    divergence = (
        ahead_x[:, 0]
        - behind_x[:, 0]
        + (ahead_y[:, 1] - behind_y[:, 1])
        + (ahead_z[:, 2] - behind_z[:, 2])
    ) * half_inverse
    coupling = jnp.stack([grad_x, grad_y, grad_z, divergence], axis=1)
    result = 2.0 * metric[:, None] * (center - earlier) + laplace + coupling
    if pinned is None:
        return result
    return jnp.where(pinned > 0, center, result)


def diagonal_of(metric, spacing, pinned):
    diagonal = 2.0 * metric[:, None] + 6.0 / (spacing * spacing)
    if pinned is None:
        return diagonal
    return jnp.where(pinned > 0, 1.0, diagonal)


def build_pinned(wall_mask):
    moving = (wall_mask > 0).astype(jnp.int32)
    walled = (wall_mask == 1).astype(jnp.int32)
    return jnp.stack([moving, walled, walled, jnp.zeros_like(walled)], axis=0)[None]


def pair_matrix(wide):
    fine = lax.broadcasted_iota(jnp.int32, (wide, wide // 2), 0)
    coarse = lax.broadcasted_iota(jnp.int32, (wide, wide // 2), 1)
    return (fine // 2 == coarse).astype(jnp.float32)


def restrict(values):
    summed = values[..., 0::2, :, :] + values[..., 1::2, :, :]
    summed = summed[..., 0::2, :] + summed[..., 1::2, :]
    summed = jnp.einsum(
        "...z,zw->...w", summed, pair_matrix(summed.shape[-1]), precision=lax.Precision.HIGHEST
    )
    return summed * 0.125


def prolong(values):
    spread = jnp.einsum(
        "...w,zw->...z",
        values,
        pair_matrix(2 * values.shape[-1]),
        precision=lax.Precision.HIGHEST,
    )
    spread = jnp.repeat(spread, 2, axis=-2)
    return jnp.repeat(spread, 2, axis=-3)


def coarse_kernel(src_ref, met_ref, out_ref, *, spacing, depth_x, height_y, width_z):
    steps, rows, lanes = src_ref.shape
    inverse_square = 1.0 / (spacing * spacing)
    half_inverse = 0.5 / spacing
    row = lax.broadcasted_iota(jnp.int32, (rows, lanes), 0)
    lane = lax.broadcasted_iota(jnp.int32, (rows, lanes), 1)
    plane = row % depth_x
    part = row // depth_x
    across_z = lane % width_z
    across_y = lane // width_z
    quarter = rows // 4
    zero = jnp.zeros((rows, lanes), jnp.float32)

    def shifted(v, shift, axis, edge):
        size = v.shape[axis]
        return jnp.where(edge, zero, pltpu.roll(v, shift % size, axis))

    def apply(v, two_g):
        ahead_x = shifted(v, -1, 0, plane == depth_x - 1)
        behind_x = shifted(v, 1, 0, plane == 0)
        ahead_y = shifted(v, -width_z, 1, across_y == height_y - 1)
        behind_y = shifted(v, width_z, 1, across_y == 0)
        ahead_z = shifted(v, -1, 1, across_z == width_z - 1)
        behind_z = shifted(v, 1, 1, across_z == 0)
        laplace = (6.0 * v - ahead_x - behind_x - ahead_y - behind_y - ahead_z - behind_z) * inverse_square
        diff_x = ahead_x - behind_x
        diff_y = ahead_y - behind_y
        diff_z = ahead_z - behind_z
        grad_x = pltpu.roll(diff_x, quarter, 0)
        grad_y = pltpu.roll(diff_y, 2 * quarter, 0)
        grad_z = pltpu.roll(diff_z, 3 * quarter, 0)
        divergence = pltpu.roll(diff_x, 3 * quarter, 0) + pltpu.roll(diff_y, 2 * quarter, 0) + pltpu.roll(diff_z, quarter, 0)
        coupling = jnp.where(part == 0, grad_x, jnp.where(part == 1, grad_y, jnp.where(part == 2, grad_z, divergence))) * half_inverse
        return two_g * v + laplace + coupling

    def advance(t, earlier):
        g = met_ref[t]
        two_g = 2.0 * g
        diagonal = two_g + 6.0 / (spacing * spacing)
        target = src_ref[t] + two_g * earlier
        v = zero
        for repeat in range(COARSE_SWEEPS):
            v = v + (target - apply(v, two_g)) / diagonal
        out_ref[t] = v
        return v

    lax.fori_loop(0, steps, advance, zero)


def coarse_solve(source, metric, spacing):
    steps, components, depth_x, height_y, width_z = source.shape
    rows = components * depth_x
    lanes = height_y * width_z
    flat_source = source.reshape(steps, rows, lanes)
    flat_metric = jnp.tile(metric.reshape(steps, depth_x, lanes), (1, components, 1))
    kernel = functools.partial(coarse_kernel, spacing=spacing, depth_x=depth_x, height_y=height_y, width_z=width_z)
    solved = pl.pallas_call(
        kernel,
        out_shape=jax.ShapeDtypeStruct(flat_source.shape, jnp.float32),
    )(flat_source, flat_metric)
    return solved.reshape(source.shape)


def apply_local(values, metric, spacing, pinned):
    padded = with_halo(values, (("space", 2),), 1)
    arrived = from_behind(values, "tm", 1)
    earlier = jnp.concatenate([arrived, values[:-1]], axis=0)
    return stencil_apply(padded, metric, earlier, spacing, pinned)


def assemble(flat_source, flat_metric, time_devs, plane_devs, local_dims):
    local_steps, components, planes, height_y, width_z = local_dims
    whole_source = flat_source.reshape(
        time_devs, plane_devs, local_steps, components, planes, height_y, width_z
    )
    whole_source = whole_source.transpose(0, 2, 3, 1, 4, 5, 6).reshape(
        time_devs * local_steps, components, plane_devs * planes, height_y, width_z
    )
    whole_metric = flat_metric.reshape(
        time_devs, plane_devs, local_steps, planes, height_y, width_z
    )
    whole_metric = whole_metric.transpose(0, 2, 1, 3, 4, 5).reshape(
        time_devs * local_steps, plane_devs * planes, height_y, width_z
    )
    return (whole_source, whole_metric)


def gather_all(flat):
    within = lax.all_gather(flat, "space", axis=0, tiled=True)
    return lax.all_gather(within, "tm", axis=0, tiled=True)


def coarse_correction(source, metric_two, gathered):
    time_devs = lax.axis_size("tm")
    plane_devs = lax.axis_size("space")
    time_at = lax.axis_index("tm")
    plane_at = lax.axis_index("space")
    local_dims = source.shape
    local_steps, components, planes, height_y, width_z = local_dims
    source_flat = source.reshape(1, -1)
    cut = source_flat.shape[1]
    if "metric" in gathered:
        flat_source = gather_all(source_flat)
        flat_metric = gathered["metric"]
    else:
        both = jnp.concatenate([source_flat, metric_two.reshape(1, -1)], axis=1)
        flat_both = gather_all(both)
        flat_source = flat_both[:, :cut]
        flat_metric = flat_both[:, cut:]
        gathered["metric"] = flat_metric
    whole_source, whole_metric = assemble(
        flat_source, flat_metric, time_devs, plane_devs, local_dims
    )
    solved = coarse_solve(whole_source, whole_metric, 4.0)
    return lax.dynamic_slice(
        solved,
        (time_at * local_steps, 0, plane_at * planes, 0, 0),
        (local_steps, components, planes, height_y, width_z),
    )


def per_device(right_side, metric, wall_mask):
    pinned = build_pinned(wall_mask)
    metric_one = restrict(metric)
    metric_two = restrict(metric_one)
    metrics = (metric, metric_one)
    pinned_levels = (pinned, None)
    gathered = {}

    def cycle(depth, values, source):
        spacing = 2.0**depth
        diagonal = diagonal_of(metrics[depth], spacing, pinned_levels[depth])
        for repeat in range(NU):
            values = (
                values
                + OMEGA
                * (source - apply_local(values, metrics[depth], spacing, pinned_levels[depth]))
                / diagonal
            )
        residual = source - apply_local(values, metrics[depth], spacing, pinned_levels[depth])
        coarse_source = restrict(residual)
        if depth == 1:
            correction = coarse_correction(coarse_source, metric_two, gathered)
        else:
            correction = cycle(1, jnp.zeros_like(coarse_source), coarse_source)
        values = values + prolong(correction)
        for repeat in range(NU):
            values = (
                values
                + OMEGA
                * (source - apply_local(values, metrics[depth], spacing, pinned_levels[depth]))
                / diagonal
            )
        return values

    solution = jnp.zeros_like(right_side)
    for repeat in range(CYCLES):
        solution = cycle(0, solution, right_side)
    return solution


def solution(mesh):
    placed = (
        P("tm", None, "space", None, None),
        P("tm", "space", None, None),
        P("space", None, None),
    )
    return jax.shard_map(
        per_device,
        mesh=mesh,
        in_specs=placed,
        out_specs=P("tm", None, "space", None, None),
        check_vma=False,
    )
```

```python
import functools

import jax
import jax.numpy as jnp
from jax import lax
from jax.experimental import pallas as pl
from jax.experimental.pallas import tpu as pltpu
from jax.sharding import PartitionSpec as P

CYCLES = 2
NU = 2
COARSE_SWEEPS = 4


OMEGA = 0.6


def with_halo(block, sides, width):
    for axis, dim in sides:
        count = lax.axis_size(axis)
        forward = [(i, i + 1) for i in range(count - 1)]
        backward = [(target, source) for source, target in forward]
        low = lax.ppermute(
            lax.slice_in_dim(block, block.shape[dim] - width, None, axis=dim), axis, forward
        )
        high = lax.ppermute(lax.slice_in_dim(block, 0, width, axis=dim), axis, backward)
        block = jnp.concatenate([low, block, high], axis=dim)
    return block


def from_behind(array, axis, by):
    size = lax.axis_size(axis)
    pairs = [(i, i + by) for i in range(size) if 0 <= i + by < size]
    return lax.ppermute(array, axis, pairs)


def stencil_apply(padded, metric, earlier, spacing, pinned):
    center = padded[:, :, 1:-1]
    ahead_x = padded[:, :, 2:]
    behind_x = padded[:, :, :-2]
    padded_yz = jnp.pad(center, ((0, 0), (0, 0), (0, 0), (1, 1), (1, 1)))
    ahead_y = padded_yz[:, :, :, 2:, 1:-1]
    behind_y = padded_yz[:, :, :, :-2, 1:-1]
    ahead_z = padded_yz[:, :, :, 1:-1, 2:]
    behind_z = padded_yz[:, :, :, 1:-1, :-2]
    inverse_square = 1.0 / (spacing * spacing)
    half_inverse = 0.5 / spacing
    laplace = (
        6.0 * center - ahead_x - behind_x - ahead_y - behind_y - ahead_z - behind_z
    ) * inverse_square
    grad_x = (ahead_x[:, 3] - behind_x[:, 3]) * half_inverse
    grad_y = (ahead_y[:, 3] - behind_y[:, 3]) * half_inverse
    grad_z = (ahead_z[:, 3] - behind_z[:, 3]) * half_inverse
    divergence = (
        ahead_x[:, 0]
        - behind_x[:, 0]
        + (ahead_y[:, 1] - behind_y[:, 1])
        + (ahead_z[:, 2] - behind_z[:, 2])
    ) * half_inverse
    coupling = jnp.stack([grad_x, grad_y, grad_z, divergence], axis=1)
    result = 2.0 * metric[:, None] * (center - earlier) + laplace + coupling
    if pinned is None:
        return result
    return jnp.where(pinned > 0, center, result)


def diagonal_of(metric, spacing, pinned):
    diagonal = 2.0 * metric[:, None] + 6.0 / (spacing * spacing)
    if pinned is None:
        return diagonal
    return jnp.where(pinned > 0, 1.0, diagonal)


def build_pinned(wall_mask):
    moving = (wall_mask > 0).astype(jnp.int32)
    walled = (wall_mask == 1).astype(jnp.int32)
    return jnp.stack([moving, walled, walled, jnp.zeros_like(walled)], axis=0)[None]


def pair_matrix(wide):
    fine = lax.broadcasted_iota(jnp.int32, (wide, wide // 2), 0)
    coarse = lax.broadcasted_iota(jnp.int32, (wide, wide // 2), 1)
    return (fine // 2 == coarse).astype(jnp.float32)


def restrict(values):
    summed = values[..., 0::2, :, :] + values[..., 1::2, :, :]
    summed = summed[..., 0::2, :] + summed[..., 1::2, :]
    summed = jnp.einsum(
        "...z,zw->...w", summed, pair_matrix(summed.shape[-1]), precision=lax.Precision.HIGHEST
    )
    return summed * 0.125


def prolong(values):
    spread = jnp.einsum(
        "...w,zw->...z",
        values,
        pair_matrix(2 * values.shape[-1]),
        precision=lax.Precision.HIGHEST,
    )
    spread = jnp.repeat(spread, 2, axis=-2)
    return jnp.repeat(spread, 2, axis=-3)


def coarse_kernel(src_ref, met_ref, out_ref, *, spacing, components, height_y, width_z):
    steps, rows, lanes = src_ref.shape
    depth_x = rows // components
    inverse_square = 1.0 / (spacing * spacing)
    half_inverse = 0.5 / spacing
    row = lax.broadcasted_iota(jnp.int32, (rows, lanes), 0)
    lane = lax.broadcasted_iota(jnp.int32, (rows, lanes), 1)
    plane = row // components
    part = row % components
    across_z = lane % width_z
    across_y = lane // width_z
    zero = jnp.zeros((rows, lanes), jnp.float32)

    def rolled(v, shift, axis):
        return pltpu.roll(v, shift % v.shape[axis], axis)

    def shifted(v, shift, axis, edge):
        return jnp.where(edge, zero, rolled(v, shift, axis))

    def apply(v, two_g):
        ahead_x = shifted(v, -components, 0, plane == depth_x - 1)
        behind_x = shifted(v, components, 0, plane == 0)
        ahead_y = shifted(v, -width_z, 1, across_y == height_y - 1)
        behind_y = shifted(v, width_z, 1, across_y == 0)
        ahead_z = shifted(v, -1, 1, across_z == width_z - 1)
        behind_z = shifted(v, 1, 1, across_z == 0)
        laplace = (6.0 * v - ahead_x - behind_x - ahead_y - behind_y - ahead_z - behind_z) * inverse_square
        diff_x = ahead_x - behind_x
        diff_y = ahead_y - behind_y
        diff_z = ahead_z - behind_z
        grad_x = rolled(diff_x, -3, 0)
        grad_y = rolled(diff_y, -2, 0)
        grad_z = rolled(diff_z, -1, 0)
        divergence = rolled(diff_x, 3, 0) + rolled(diff_y, 2, 0) + rolled(diff_z, 1, 0)
        coupling = jnp.where(part == 0, grad_x, jnp.where(part == 1, grad_y, jnp.where(part == 2, grad_z, divergence))) * half_inverse
        return two_g * v + laplace + coupling

    def advance(t, earlier):
        g = met_ref[t]
        two_g = 2.0 * g
        diagonal = two_g + 6.0 / (spacing * spacing)
        target = src_ref[t] + two_g * earlier
        v = zero
        for repeat in range(COARSE_SWEEPS):
            v = v + (target - apply(v, two_g)) / diagonal
        out_ref[t] = v
        return v

    lax.fori_loop(0, steps, advance, zero)


def coarse_solve(flat_source, flat_metric, spacing, components, height_y, width_z):
    kernel = functools.partial(
        coarse_kernel, spacing=spacing, components=components, height_y=height_y, width_z=width_z
    )
    return pl.pallas_call(
        kernel,
        out_shape=jax.ShapeDtypeStruct(flat_source.shape, jnp.float32),
    )(flat_source, jnp.repeat(flat_metric, components, axis=1))


def apply_local(values, metric, spacing, pinned):
    padded = with_halo(values, (("space", 2),), 1)
    arrived = from_behind(values, "tm", 1)
    earlier = jnp.concatenate([arrived, values[:-1]], axis=0)
    return stencil_apply(padded, metric, earlier, spacing, pinned)


def assemble(flat_source, flat_metric, time_devs, plane_devs, local_dims):
    local_steps, components, planes, height_y, width_z = local_dims
    lanes = height_y * width_z
    whole_source = flat_source.reshape(
        time_devs, plane_devs, local_steps, components, planes, lanes
    )
    whole_source = whole_source.transpose(0, 2, 1, 4, 3, 5).reshape(
        time_devs * local_steps, plane_devs * planes * components, lanes
    )
    whole_metric = flat_metric.reshape(time_devs, plane_devs, local_steps, planes, lanes)
    whole_metric = whole_metric.transpose(0, 2, 1, 3, 4).reshape(
        time_devs * local_steps, plane_devs * planes, lanes
    )
    return (whole_source, whole_metric)


def gather_all(flat):
    within = lax.all_gather(flat, "space", axis=0, tiled=True)
    return lax.all_gather(within, "tm", axis=0, tiled=True)


def coarse_correction(source, metric_two, gathered):
    time_devs = lax.axis_size("tm")
    plane_devs = lax.axis_size("space")
    time_at = lax.axis_index("tm")
    plane_at = lax.axis_index("space")
    local_dims = source.shape
    local_steps, components, planes, height_y, width_z = local_dims
    source_flat = source.reshape(1, -1)
    cut = source_flat.shape[1]
    if "metric" in gathered:
        flat_source = gather_all(source_flat)
        flat_metric = gathered["metric"]
    else:
        both = jnp.concatenate([source_flat, metric_two.reshape(1, -1)], axis=1)
        flat_both = gather_all(both)
        flat_source = flat_both[:, :cut]
        flat_metric = flat_both[:, cut:]
        gathered["metric"] = flat_metric
    whole_source, whole_metric = assemble(
        flat_source, flat_metric, time_devs, plane_devs, local_dims
    )
    solved = coarse_solve(whole_source, whole_metric, 4.0, components, height_y, width_z)
    mine = lax.dynamic_slice(
        solved,
        (time_at * local_steps, plane_at * planes * components, 0),
        (local_steps, planes * components, height_y * width_z),
    )
    mine = mine.reshape(local_steps, planes, components, height_y, width_z)
    return mine.transpose(0, 2, 1, 3, 4)


def per_device(right_side, metric, wall_mask):
    pinned = build_pinned(wall_mask)
    metric_one = restrict(metric)
    metric_two = restrict(metric_one)
    metrics = (metric, metric_one)
    pinned_levels = (pinned, None)
    gathered = {}

    def cycle(depth, values, source):
        spacing = 2.0**depth
        diagonal = diagonal_of(metrics[depth], spacing, pinned_levels[depth])
        for repeat in range(NU):
            values = (
                values
                + OMEGA
                * (source - apply_local(values, metrics[depth], spacing, pinned_levels[depth]))
                / diagonal
            )
        residual = source - apply_local(values, metrics[depth], spacing, pinned_levels[depth])
        coarse_source = restrict(residual)
        if depth == 1:
            correction = coarse_correction(coarse_source, metric_two, gathered)
        else:
            correction = cycle(1, jnp.zeros_like(coarse_source), coarse_source)
        values = values + prolong(correction)
        for repeat in range(NU):
            values = (
                values
                + OMEGA
                * (source - apply_local(values, metrics[depth], spacing, pinned_levels[depth]))
                / diagonal
            )
        return values

    solution = jnp.zeros_like(right_side)
    for repeat in range(CYCLES):
        solution = cycle(0, solution, right_side)
    return solution


def solution(mesh):
    placed = (
        P("tm", None, "space", None, None),
        P("tm", "space", None, None),
        P("space", None, None),
    )
    return jax.shard_map(
        per_device,
        mesh=mesh,
        in_specs=placed,
        out_specs=P("tm", None, "space", None, None),
        check_vma=False,
    )
```

```python
import functools

import jax
import jax.numpy as jnp
from jax import lax
from jax.experimental import pallas as pl
from jax.experimental.pallas import tpu as pltpu
from jax.sharding import PartitionSpec as P

CYCLES = 2
NU = 2
COARSE_SWEEPS = 4


OMEGA = 0.6


def with_halo(block, sides, width):
    for axis, dim in sides:
        count = lax.axis_size(axis)
        forward = [(i, i + 1) for i in range(count - 1)]
        backward = [(target, source) for source, target in forward]
        low = lax.ppermute(
            lax.slice_in_dim(block, block.shape[dim] - width, None, axis=dim), axis, forward
        )
        high = lax.ppermute(lax.slice_in_dim(block, 0, width, axis=dim), axis, backward)
        block = jnp.concatenate([low, block, high], axis=dim)
    return block


def from_behind(array, axis, by):
    size = lax.axis_size(axis)
    pairs = [(i, i + by) for i in range(size) if 0 <= i + by < size]
    return lax.ppermute(array, axis, pairs)


def stencil_apply(padded, metric, earlier, spacing, pinned):
    center = padded[:, :, 1:-1]
    ahead_x = padded[:, :, 2:]
    behind_x = padded[:, :, :-2]
    padded_yz = jnp.pad(center, ((0, 0), (0, 0), (0, 0), (1, 1), (1, 1)))
    ahead_y = padded_yz[:, :, :, 2:, 1:-1]
    behind_y = padded_yz[:, :, :, :-2, 1:-1]
    ahead_z = padded_yz[:, :, :, 1:-1, 2:]
    behind_z = padded_yz[:, :, :, 1:-1, :-2]
    inverse_square = 1.0 / (spacing * spacing)
    half_inverse = 0.5 / spacing
    laplace = (
        6.0 * center - ahead_x - behind_x - ahead_y - behind_y - ahead_z - behind_z
    ) * inverse_square
    grad_x = (ahead_x[:, 3] - behind_x[:, 3]) * half_inverse
    grad_y = (ahead_y[:, 3] - behind_y[:, 3]) * half_inverse
    grad_z = (ahead_z[:, 3] - behind_z[:, 3]) * half_inverse
    divergence = (
        ahead_x[:, 0]
        - behind_x[:, 0]
        + (ahead_y[:, 1] - behind_y[:, 1])
        + (ahead_z[:, 2] - behind_z[:, 2])
    ) * half_inverse
    coupling = jnp.stack([grad_x, grad_y, grad_z, divergence], axis=1)
    result = 2.0 * metric[:, None] * (center - earlier) + laplace + coupling
    if pinned is None:
        return result
    return jnp.where(pinned > 0, center, result)


def diagonal_of(metric, spacing, pinned):
    diagonal = 2.0 * metric[:, None] + 6.0 / (spacing * spacing)
    if pinned is None:
        return diagonal
    return jnp.where(pinned > 0, 1.0, diagonal)


def build_pinned(wall_mask):
    moving = (wall_mask > 0).astype(jnp.int32)
    walled = (wall_mask == 1).astype(jnp.int32)
    return jnp.stack([moving, walled, walled, jnp.zeros_like(walled)], axis=0)[None]


def pair_matrix(wide):
    fine = lax.broadcasted_iota(jnp.int32, (wide, wide // 2), 0)
    coarse = lax.broadcasted_iota(jnp.int32, (wide, wide // 2), 1)
    return (fine // 2 == coarse).astype(jnp.float32)


def restrict(values):
    summed = values[..., 0::2, :, :] + values[..., 1::2, :, :]
    summed = summed[..., 0::2, :] + summed[..., 1::2, :]
    summed = jnp.einsum(
        "...z,zw->...w", summed, pair_matrix(summed.shape[-1]), precision=lax.Precision.HIGHEST
    )
    return summed * 0.125


def prolong(values):
    spread = jnp.einsum(
        "...w,zw->...z",
        values,
        pair_matrix(2 * values.shape[-1]),
        precision=lax.Precision.HIGHEST,
    )
    spread = jnp.repeat(spread, 2, axis=-2)
    return jnp.repeat(spread, 2, axis=-3)


def coarse_kernel(src_ref, met_ref, out_ref, *, spacing, components, height_y, width_z):
    steps, rows, lanes = src_ref.shape
    depth_x = rows // components
    inverse_square = 1.0 / (spacing * spacing)
    half_inverse = 0.5 / spacing
    row = lax.broadcasted_iota(jnp.int32, (rows, lanes), 0)
    lane = lax.broadcasted_iota(jnp.int32, (rows, lanes), 1)
    plane = row // components
    part = row % components
    across_z = lane % width_z
    across_y = lane // width_z
    zero = jnp.zeros((rows, lanes), jnp.float32)

    def rolled(v, shift, axis):
        return pltpu.roll(v, shift % v.shape[axis], axis)

    def shifted(v, shift, axis, edge):
        return jnp.where(edge, zero, rolled(v, shift, axis))

    def apply(v, two_g):
        ahead_x = shifted(v, -components, 0, plane == depth_x - 1)
        behind_x = shifted(v, components, 0, plane == 0)
        ahead_y = shifted(v, -width_z, 1, across_y == height_y - 1)
        behind_y = shifted(v, width_z, 1, across_y == 0)
        ahead_z = shifted(v, -1, 1, across_z == width_z - 1)
        behind_z = shifted(v, 1, 1, across_z == 0)
        laplace = (6.0 * v - ahead_x - behind_x - ahead_y - behind_y - ahead_z - behind_z) * inverse_square
        diff_x = ahead_x - behind_x
        diff_y = ahead_y - behind_y
        diff_z = ahead_z - behind_z
        grad_x = rolled(diff_x, -3, 0)
        grad_y = rolled(diff_y, -2, 0)
        grad_z = rolled(diff_z, -1, 0)
        divergence = rolled(diff_x, 3, 0) + rolled(diff_y, 2, 0) + rolled(diff_z, 1, 0)
        coupling = jnp.where(part == 0, grad_x, jnp.where(part == 1, grad_y, jnp.where(part == 2, grad_z, divergence))) * half_inverse
        return two_g * v + laplace + coupling

    def advance(t, earlier):
        g = met_ref[t]
        two_g = 2.0 * g
        diagonal = two_g + 6.0 / (spacing * spacing)
        target = src_ref[t] + two_g * earlier
        v = zero
        for repeat in range(COARSE_SWEEPS):
            v = v + (target - apply(v, two_g)) / diagonal
        out_ref[t] = v
        return v

    lax.fori_loop(0, steps, advance, zero)


def coarse_solve(flat_source, flat_metric, spacing, components, height_y, width_z):
    kernel = functools.partial(
        coarse_kernel, spacing=spacing, components=components, height_y=height_y, width_z=width_z
    )
    return pl.pallas_call(
        kernel,
        out_shape=jax.ShapeDtypeStruct(flat_source.shape, jnp.float32),
    )(flat_source, jnp.repeat(flat_metric, components, axis=1))


def apply_local(values, metric, spacing, pinned):
    padded = with_halo(values, (("space", 2),), 1)
    arrived = from_behind(values, "tm", 1)
    earlier = jnp.concatenate([arrived, values[:-1]], axis=0)
    return stencil_apply(padded, metric, earlier, spacing, pinned)


def assemble(flat_source, flat_metric, time_devs, plane_devs, local_dims):
    local_steps, components, planes, height_y, width_z = local_dims
    lanes = height_y * width_z
    whole_source = flat_source.reshape(
        time_devs, plane_devs, local_steps, components, planes, lanes
    )
    whole_source = whole_source.transpose(0, 2, 1, 4, 3, 5).reshape(
        time_devs * local_steps, plane_devs * planes * components, lanes
    )
    whole_metric = flat_metric.reshape(time_devs, plane_devs, local_steps, planes, lanes)
    whole_metric = whole_metric.transpose(0, 2, 1, 3, 4).reshape(
        time_devs * local_steps, plane_devs * planes, lanes
    )
    return (whole_source, whole_metric)


def gather_all(flat):
    within = lax.all_gather(flat, "space", axis=0, tiled=True)
    return lax.all_gather(within, "tm", axis=0, tiled=True)


def coarse_correction(source, metric_two, gathered):
    time_devs = lax.axis_size("tm")
    plane_devs = lax.axis_size("space")
    time_at = lax.axis_index("tm")
    plane_at = lax.axis_index("space")
    local_dims = source.shape
    local_steps, components, planes, height_y, width_z = local_dims
    source_flat = source.reshape(1, -1)
    cut = source_flat.shape[1]
    if "metric" in gathered:
        flat_source = gather_all(source_flat)
        flat_metric = gathered["metric"]
    else:
        both = jnp.concatenate([source_flat, metric_two.reshape(1, -1)], axis=1)
        flat_both = gather_all(both)
        flat_source = flat_both[:, :cut]
        flat_metric = flat_both[:, cut:]
        gathered["metric"] = flat_metric
    whole_source, whole_metric = assemble(
        flat_source, flat_metric, time_devs, plane_devs, local_dims
    )
    solved = coarse_solve(whole_source, whole_metric, 4.0, components, height_y, width_z)
    mine = lax.dynamic_slice(
        solved,
        (time_at * local_steps, plane_at * planes * components, 0),
        (local_steps, planes * components, height_y * width_z),
    )
    mine = mine.reshape(local_steps, planes, components, height_y, width_z)
    return mine.transpose(0, 2, 1, 3, 4)


def per_device(right_side, metric, wall_mask):
    pinned = build_pinned(wall_mask)
    metric_one = restrict(metric)
    metric_two = restrict(metric_one)
    metrics = (metric, metric_one)
    pinned_levels = (pinned, None)
    gathered = {}

    def sweep(depth, values, source, diagonal):
        if values is None:
            return OMEGA * source / diagonal
        spacing = 2.0**depth
        applied = apply_local(values, metrics[depth], spacing, pinned_levels[depth])
        return values + OMEGA * (source - applied) / diagonal

    def cycle(depth, values, source):
        spacing = 2.0**depth
        diagonal = diagonal_of(metrics[depth], spacing, pinned_levels[depth])
        for repeat in range(NU):
            values = sweep(depth, values, source, diagonal)
        residual = source - apply_local(values, metrics[depth], spacing, pinned_levels[depth])
        coarse_source = restrict(residual)
        if depth == 1:
            correction = coarse_correction(coarse_source, metric_two, gathered)
        else:
            correction = cycle(1, None, coarse_source)
        values = values + prolong(correction)
        for repeat in range(NU):
            values = sweep(depth, values, source, diagonal)
        return values

    solution = None
    for repeat in range(CYCLES):
        solution = cycle(0, solution, right_side)
    return solution


def solution(mesh):
    placed = (
        P("tm", None, "space", None, None),
        P("tm", "space", None, None),
        P("space", None, None),
    )
    return jax.shard_map(
        per_device,
        mesh=mesh,
        in_specs=placed,
        out_specs=P("tm", None, "space", None, None),
        check_vma=False,
    )
```

```python
import functools

import jax
import jax.numpy as jnp
from jax import lax
from jax.experimental import pallas as pl
from jax.experimental.pallas import tpu as pltpu
from jax.sharding import PartitionSpec as P

CYCLES = 2
NU = 2
COARSE_SWEEPS = 4


OMEGA = 0.6


def with_halo(block, sides, width):
    for axis, dim in sides:
        count = lax.axis_size(axis)
        forward = [(i, i + 1) for i in range(count - 1)]
        backward = [(target, source) for source, target in forward]
        low = lax.ppermute(
            lax.slice_in_dim(block, block.shape[dim] - width, None, axis=dim), axis, forward
        )
        high = lax.ppermute(lax.slice_in_dim(block, 0, width, axis=dim), axis, backward)
        block = jnp.concatenate([low, block, high], axis=dim)
    return block


def from_behind(array, axis, by):
    size = lax.axis_size(axis)
    pairs = [(i, i + by) for i in range(size) if 0 <= i + by < size]
    return lax.ppermute(array, axis, pairs)


def stencil_apply(padded, metric, earlier, spacing, pinned):
    center = padded[:, :, 1:-1]
    ahead_x = padded[:, :, 2:]
    behind_x = padded[:, :, :-2]
    padded_yz = jnp.pad(center, ((0, 0), (0, 0), (0, 0), (1, 1), (1, 1)))
    ahead_y = padded_yz[:, :, :, 2:, 1:-1]
    behind_y = padded_yz[:, :, :, :-2, 1:-1]
    ahead_z = padded_yz[:, :, :, 1:-1, 2:]
    behind_z = padded_yz[:, :, :, 1:-1, :-2]
    inverse_square = 1.0 / (spacing * spacing)
    half_inverse = 0.5 / spacing
    laplace = (
        6.0 * center - ahead_x - behind_x - ahead_y - behind_y - ahead_z - behind_z
    ) * inverse_square
    grad_x = (ahead_x[:, 3] - behind_x[:, 3]) * half_inverse
    grad_y = (ahead_y[:, 3] - behind_y[:, 3]) * half_inverse
    grad_z = (ahead_z[:, 3] - behind_z[:, 3]) * half_inverse
    divergence = (
        ahead_x[:, 0]
        - behind_x[:, 0]
        + (ahead_y[:, 1] - behind_y[:, 1])
        + (ahead_z[:, 2] - behind_z[:, 2])
    ) * half_inverse
    coupling = jnp.stack([grad_x, grad_y, grad_z, divergence], axis=1)
    result = 2.0 * metric[:, None] * (center - earlier) + laplace + coupling
    if pinned is None:
        return result
    return jnp.where(pinned > 0, center, result)


def diagonal_of(metric, spacing, pinned):
    diagonal = 2.0 * metric[:, None] + 6.0 / (spacing * spacing)
    if pinned is None:
        return diagonal
    return jnp.where(pinned > 0, 1.0, diagonal)


def build_pinned(wall_mask):
    moving = (wall_mask > 0).astype(jnp.int32)
    walled = (wall_mask == 1).astype(jnp.int32)
    return jnp.stack([moving, walled, walled, jnp.zeros_like(walled)], axis=0)[None]


def pair_matrix(wide):
    fine = lax.broadcasted_iota(jnp.int32, (wide, wide // 2), 0)
    coarse = lax.broadcasted_iota(jnp.int32, (wide, wide // 2), 1)
    return (fine // 2 == coarse).astype(jnp.float32)


def restrict(values):
    summed = values[..., 0::2, :, :] + values[..., 1::2, :, :]
    summed = summed[..., 0::2, :] + summed[..., 1::2, :]
    summed = jnp.einsum(
        "...z,zw->...w", summed, pair_matrix(summed.shape[-1]), precision=lax.Precision.HIGHEST
    )
    return summed * 0.125


def prolong(values):
    spread = jnp.einsum(
        "...w,zw->...z",
        values,
        pair_matrix(2 * values.shape[-1]),
        precision=lax.Precision.HIGHEST,
    )
    spread = jnp.repeat(spread, 2, axis=-2)
    return jnp.repeat(spread, 2, axis=-3)


def coarse_kernel(src_ref, met_ref, out_ref, *, spacing, components, height_y, width_z):
    steps, rows, lanes = src_ref.shape
    depth_x = rows // components
    inverse_square = 1.0 / (spacing * spacing)
    half_inverse = 0.5 / spacing
    row = lax.broadcasted_iota(jnp.int32, (rows, lanes), 0)
    lane = lax.broadcasted_iota(jnp.int32, (rows, lanes), 1)
    plane = row // components
    part = row % components
    across_z = lane % width_z
    across_y = lane // width_z
    zero = jnp.zeros((rows, lanes), jnp.float32)

    def rolled(v, shift, axis):
        return pltpu.roll(v, shift % v.shape[axis], axis)

    def shifted(v, shift, axis, edge):
        return jnp.where(edge, zero, rolled(v, shift, axis))

    def apply(v, two_g):
        ahead_x = shifted(v, -components, 0, plane == depth_x - 1)
        behind_x = shifted(v, components, 0, plane == 0)
        ahead_y = shifted(v, -width_z, 1, across_y == height_y - 1)
        behind_y = shifted(v, width_z, 1, across_y == 0)
        ahead_z = shifted(v, -1, 1, across_z == width_z - 1)
        behind_z = shifted(v, 1, 1, across_z == 0)
        laplace = (6.0 * v - ahead_x - behind_x - ahead_y - behind_y - ahead_z - behind_z) * inverse_square
        diff_x = ahead_x - behind_x
        diff_y = ahead_y - behind_y
        diff_z = ahead_z - behind_z
        grad_x = rolled(diff_x, -3, 0)
        grad_y = rolled(diff_y, -2, 0)
        grad_z = rolled(diff_z, -1, 0)
        divergence = rolled(diff_x, 3, 0) + rolled(diff_y, 2, 0) + rolled(diff_z, 1, 0)
        coupling = jnp.where(part == 0, grad_x, jnp.where(part == 1, grad_y, jnp.where(part == 2, grad_z, divergence))) * half_inverse
        return two_g * v + laplace + coupling

    def advance(t, earlier):
        g = met_ref[t]
        two_g = 2.0 * g
        diagonal = two_g + 6.0 / (spacing * spacing)
        target = src_ref[t] + two_g * earlier
        v = zero
        for repeat in range(COARSE_SWEEPS):
            v = v + (target - apply(v, two_g)) / diagonal
        out_ref[t] = v
        return v

    lax.fori_loop(0, steps, advance, zero)


def coarse_solve(flat_source, flat_metric, spacing, components, height_y, width_z):
    kernel = functools.partial(
        coarse_kernel, spacing=spacing, components=components, height_y=height_y, width_z=width_z
    )
    return pl.pallas_call(
        kernel,
        out_shape=jax.ShapeDtypeStruct(flat_source.shape, jnp.float32),
    )(flat_source, jnp.repeat(flat_metric, components, axis=1))


def apply_local(values, metric, spacing, pinned):
    padded = with_halo(values, (("space", 2),), 1)
    arrived = from_behind(values, "tm", 1)
    earlier = jnp.concatenate([arrived, values[:-1]], axis=0)
    return stencil_apply(padded, metric, earlier, spacing, pinned)


def assemble(flat_source, flat_metric, time_devs, plane_devs, local_dims):
    local_steps, components, planes, height_y, width_z = local_dims
    lanes = height_y * width_z
    whole_source = flat_source.reshape(
        time_devs, plane_devs, local_steps, components, planes, lanes
    )
    whole_source = whole_source.transpose(0, 2, 1, 4, 3, 5).reshape(
        time_devs * local_steps, plane_devs * planes * components, lanes
    )
    whole_metric = flat_metric.reshape(time_devs, plane_devs, local_steps, planes, lanes)
    whole_metric = whole_metric.transpose(0, 2, 1, 3, 4).reshape(
        time_devs * local_steps, plane_devs * planes, lanes
    )
    return (whole_source, whole_metric)


def gather_all(flat):
    within = lax.all_gather(flat, "space", axis=0, tiled=True)
    return lax.all_gather(within, "tm", axis=0, tiled=True)


def coarse_correction(source, metric_two, gathered):
    time_devs = lax.axis_size("tm")
    plane_devs = lax.axis_size("space")
    time_at = lax.axis_index("tm")
    plane_at = lax.axis_index("space")
    local_dims = source.shape
    local_steps, components, planes, height_y, width_z = local_dims
    source_flat = source.reshape(1, -1)
    cut = source_flat.shape[1]
    if "metric" in gathered:
        flat_source = gather_all(source_flat)
        flat_metric = gathered["metric"]
    else:
        both = jnp.concatenate([source_flat, metric_two.reshape(1, -1)], axis=1)
        flat_both = gather_all(both)
        flat_source = flat_both[:, :cut]
        flat_metric = flat_both[:, cut:]
        gathered["metric"] = flat_metric
    whole_source, whole_metric = assemble(
        flat_source, flat_metric, time_devs, plane_devs, local_dims
    )
    solved = coarse_solve(whole_source, whole_metric, 4.0, components, height_y, width_z)
    mine = lax.dynamic_slice(
        solved,
        (time_at * local_steps, plane_at * planes * components, 0),
        (local_steps, planes * components, height_y * width_z),
    )
    mine = mine.reshape(local_steps, planes, components, height_y, width_z)
    padded = jnp.pad(solved, ((1, 0), (components, components), (0, 0)))
    around = lax.dynamic_slice(
        padded,
        (time_at * local_steps, plane_at * planes * components, 0),
        (local_steps + 1, (planes + 2) * components, height_y * width_z),
    )
    around = around.reshape(local_steps + 1, planes + 2, components, height_y, width_z)
    fine = prolong(around.transpose(0, 2, 1, 3, 4))[:, :, 1:-1]
    return (mine.transpose(0, 2, 1, 3, 4), fine)


def per_device(right_side, metric, wall_mask):
    pinned = build_pinned(wall_mask)
    metric_one = restrict(metric)
    metric_two = restrict(metric_one)
    metrics = (metric, metric_one)
    pinned_levels = (pinned, None)
    gathered = {}

    def sweep(depth, values, source, diagonal):
        if values is None:
            return OMEGA * source / diagonal
        spacing = 2.0**depth
        applied = apply_local(values, metrics[depth], spacing, pinned_levels[depth])
        return values + OMEGA * (source - applied) / diagonal

    def cycle(depth, values, source):
        spacing = 2.0**depth
        diagonal = diagonal_of(metrics[depth], spacing, pinned_levels[depth])
        for repeat in range(NU):
            values = sweep(depth, values, source, diagonal)
        applied = apply_local(values, metrics[depth], spacing, pinned_levels[depth])
        residual = source - applied
        coarse_source = restrict(residual)
        if depth == 1:
            correction, fine = coarse_correction(coarse_source, metric_two, gathered)
            applied = applied + stencil_apply(
                fine[1:], metrics[depth], fine[:-1, :, 1:-1], spacing, None
            )
            values = values + prolong(correction)
            values = values + OMEGA * (source - applied) / diagonal
            remaining = NU - 1
        else:
            correction = cycle(1, None, coarse_source)
            values = values + prolong(correction)
            remaining = NU
        for repeat in range(remaining):
            values = sweep(depth, values, source, diagonal)
        return values

    solution = None
    for repeat in range(CYCLES):
        solution = cycle(0, solution, right_side)
    return solution


def solution(mesh):
    placed = (
        P("tm", None, "space", None, None),
        P("tm", "space", None, None),
        P("space", None, None),
    )
    return jax.shard_map(
        per_device,
        mesh=mesh,
        in_specs=placed,
        out_specs=P("tm", None, "space", None, None),
        check_vma=False,
    )
```

```python
import functools

import jax
import jax.numpy as jnp
from jax import lax
from jax.experimental import pallas as pl
from jax.experimental.pallas import tpu as pltpu
from jax.sharding import PartitionSpec as P

CYCLES = 2
NU = 2
COARSE_SWEEPS = 4


OMEGA = 0.6


def with_halo(block, sides, width):
    for axis, dim in sides:
        count = lax.axis_size(axis)
        forward = [(i, i + 1) for i in range(count - 1)]
        backward = [(target, source) for source, target in forward]
        low = lax.ppermute(
            lax.slice_in_dim(block, block.shape[dim] - width, None, axis=dim), axis, forward
        )
        high = lax.ppermute(lax.slice_in_dim(block, 0, width, axis=dim), axis, backward)
        block = jnp.concatenate([low, block, high], axis=dim)
    return block


def from_behind(array, axis, by):
    size = lax.axis_size(axis)
    pairs = [(i, i + by) for i in range(size) if 0 <= i + by < size]
    return lax.ppermute(array, axis, pairs)


def stencil_apply(padded, metric, earlier, spacing, pinned):
    center = padded[:, :, 1:-1]
    ahead_x = padded[:, :, 2:]
    behind_x = padded[:, :, :-2]
    padded_yz = jnp.pad(center, ((0, 0), (0, 0), (0, 0), (1, 1), (1, 1)))
    ahead_y = padded_yz[:, :, :, 2:, 1:-1]
    behind_y = padded_yz[:, :, :, :-2, 1:-1]
    ahead_z = padded_yz[:, :, :, 1:-1, 2:]
    behind_z = padded_yz[:, :, :, 1:-1, :-2]
    inverse_square = 1.0 / (spacing * spacing)
    half_inverse = 0.5 / spacing
    laplace = (
        6.0 * center - ahead_x - behind_x - ahead_y - behind_y - ahead_z - behind_z
    ) * inverse_square
    grad_x = (ahead_x[:, 3] - behind_x[:, 3]) * half_inverse
    grad_y = (ahead_y[:, 3] - behind_y[:, 3]) * half_inverse
    grad_z = (ahead_z[:, 3] - behind_z[:, 3]) * half_inverse
    divergence = (
        ahead_x[:, 0]
        - behind_x[:, 0]
        + (ahead_y[:, 1] - behind_y[:, 1])
        + (ahead_z[:, 2] - behind_z[:, 2])
    ) * half_inverse
    coupling = jnp.stack([grad_x, grad_y, grad_z, divergence], axis=1)
    result = 2.0 * metric[:, None] * (center - earlier) + laplace + coupling
    if pinned is None:
        return result
    return jnp.where(pinned > 0, center, result)


def diagonal_of(metric, spacing, pinned):
    diagonal = 2.0 * metric[:, None] + 6.0 / (spacing * spacing)
    if pinned is None:
        return diagonal
    return jnp.where(pinned > 0, 1.0, diagonal)


def build_pinned(wall_mask):
    moving = (wall_mask > 0).astype(jnp.int32)
    walled = (wall_mask == 1).astype(jnp.int32)
    return jnp.stack([moving, walled, walled, jnp.zeros_like(walled)], axis=0)[None]


def pair_matrix(wide):
    fine = lax.broadcasted_iota(jnp.int32, (wide, wide // 2), 0)
    coarse = lax.broadcasted_iota(jnp.int32, (wide, wide // 2), 1)
    return (fine // 2 == coarse).astype(jnp.float32)


def restrict(values):
    summed = values[..., 0::2, :, :] + values[..., 1::2, :, :]
    summed = summed[..., 0::2, :] + summed[..., 1::2, :]
    summed = jnp.einsum(
        "...z,zw->...w", summed, pair_matrix(summed.shape[-1]), precision=lax.Precision.HIGHEST
    )
    return summed * 0.125


def prolong(values):
    spread = jnp.einsum(
        "...w,zw->...z",
        values,
        pair_matrix(2 * values.shape[-1]),
        precision=lax.Precision.HIGHEST,
    )
    spread = jnp.repeat(spread, 2, axis=-2)
    return jnp.repeat(spread, 2, axis=-3)


def coarse_kernel(src_ref, met_ref, out_ref, *, spacing, components, height_y, width_z):
    steps, rows, lanes = src_ref.shape
    depth_x = rows // components
    inverse_square = 1.0 / (spacing * spacing)
    half_inverse = 0.5 / spacing
    row = lax.broadcasted_iota(jnp.int32, (rows, lanes), 0)
    lane = lax.broadcasted_iota(jnp.int32, (rows, lanes), 1)
    plane = row // components
    part = row % components
    across_z = lane % width_z
    across_y = lane // width_z
    zero = jnp.zeros((rows, lanes), jnp.float32)

    def rolled(v, shift, axis):
        return pltpu.roll(v, shift % v.shape[axis], axis)

    def shifted(v, shift, axis, edge):
        return jnp.where(edge, zero, rolled(v, shift, axis))

    def apply(v, two_g):
        ahead_x = shifted(v, -components, 0, plane == depth_x - 1)
        behind_x = shifted(v, components, 0, plane == 0)
        ahead_y = shifted(v, -width_z, 1, across_y == height_y - 1)
        behind_y = shifted(v, width_z, 1, across_y == 0)
        ahead_z = shifted(v, -1, 1, across_z == width_z - 1)
        behind_z = shifted(v, 1, 1, across_z == 0)
        laplace = (6.0 * v - ahead_x - behind_x - ahead_y - behind_y - ahead_z - behind_z) * inverse_square
        diff_x = ahead_x - behind_x
        diff_y = ahead_y - behind_y
        diff_z = ahead_z - behind_z
        grad_x = rolled(diff_x, -3, 0)
        grad_y = rolled(diff_y, -2, 0)
        grad_z = rolled(diff_z, -1, 0)
        divergence = rolled(diff_x, 3, 0) + rolled(diff_y, 2, 0) + rolled(diff_z, 1, 0)
        coupling = jnp.where(part == 0, grad_x, jnp.where(part == 1, grad_y, jnp.where(part == 2, grad_z, divergence))) * half_inverse
        return two_g * v + laplace + coupling

    def advance(t, earlier):
        g = met_ref[t]
        two_g = 2.0 * g
        diagonal = two_g + 6.0 / (spacing * spacing)
        target = src_ref[t] + two_g * earlier
        v = zero
        for repeat in range(COARSE_SWEEPS):
            v = v + (target - apply(v, two_g)) / diagonal
        out_ref[t] = v
        return v

    lax.fori_loop(0, steps, advance, zero)


def coarse_solve(flat_source, flat_metric, spacing, components, height_y, width_z):
    kernel = functools.partial(
        coarse_kernel, spacing=spacing, components=components, height_y=height_y, width_z=width_z
    )
    return pl.pallas_call(
        kernel,
        out_shape=jax.ShapeDtypeStruct(flat_source.shape, jnp.float32),
    )(flat_source, jnp.repeat(flat_metric, components, axis=1))


def apply_local(values, metric, spacing, pinned):
    padded = with_halo(values, (("space", 2),), 1)
    arrived = from_behind(values, "tm", 1)
    earlier = jnp.concatenate([arrived, values[:-1]], axis=0)
    return stencil_apply(padded, metric, earlier, spacing, pinned)


def assemble(flat_source, flat_metric, time_devs, plane_devs, local_dims):
    local_steps, components, planes, height_y, width_z = local_dims
    lanes = height_y * width_z
    whole_source = flat_source.reshape(
        time_devs, plane_devs, local_steps, components, planes, lanes
    )
    whole_source = whole_source.transpose(0, 2, 1, 4, 3, 5).reshape(
        time_devs * local_steps, plane_devs * planes * components, lanes
    )
    whole_metric = flat_metric.reshape(time_devs, plane_devs, local_steps, planes, lanes)
    whole_metric = whole_metric.transpose(0, 2, 1, 3, 4).reshape(
        time_devs * local_steps, plane_devs * planes, lanes
    )
    return (whole_source, whole_metric)


def gather_all(flat):
    across = lax.all_gather(flat, "tm", axis=0, tiled=True)
    whole = lax.all_gather(across, "space", axis=1, tiled=True)
    return whole.reshape(-1, flat.shape[1])


def coarse_correction(source, metric_two, gathered):
    time_devs = lax.axis_size("tm")
    plane_devs = lax.axis_size("space")
    time_at = lax.axis_index("tm")
    plane_at = lax.axis_index("space")
    local_dims = source.shape
    local_steps, components, planes, height_y, width_z = local_dims
    source_flat = source.reshape(1, -1)
    cut = source_flat.shape[1]
    if "metric" in gathered:
        flat_source = gather_all(source_flat)
        flat_metric = gathered["metric"]
    else:
        both = jnp.concatenate([source_flat, metric_two.reshape(1, -1)], axis=1)
        flat_both = gather_all(both)
        flat_source = flat_both[:, :cut]
        flat_metric = flat_both[:, cut:]
        gathered["metric"] = flat_metric
    whole_source, whole_metric = assemble(
        flat_source, flat_metric, time_devs, plane_devs, local_dims
    )
    solved = coarse_solve(whole_source, whole_metric, 4.0, components, height_y, width_z)
    mine = lax.dynamic_slice(
        solved,
        (time_at * local_steps, plane_at * planes * components, 0),
        (local_steps, planes * components, height_y * width_z),
    )
    mine = mine.reshape(local_steps, planes, components, height_y, width_z)
    padded = jnp.pad(solved, ((1, 0), (components, components), (0, 0)))
    around = lax.dynamic_slice(
        padded,
        (time_at * local_steps, plane_at * planes * components, 0),
        (local_steps + 1, (planes + 2) * components, height_y * width_z),
    )
    around = around.reshape(local_steps + 1, planes + 2, components, height_y, width_z)
    fine = prolong(around.transpose(0, 2, 1, 3, 4))[:, :, 1:-1]
    return (mine.transpose(0, 2, 1, 3, 4), fine)


def per_device(right_side, metric, wall_mask):
    pinned = build_pinned(wall_mask)
    metric_one = restrict(metric)
    metric_two = restrict(metric_one)
    metrics = (metric, metric_one)
    pinned_levels = (pinned, None)
    gathered = {}

    def sweep(depth, values, source, diagonal):
        if values is None:
            return OMEGA * source / diagonal
        spacing = 2.0**depth
        applied = apply_local(values, metrics[depth], spacing, pinned_levels[depth])
        return values + OMEGA * (source - applied) / diagonal

    def cycle(depth, values, source):
        spacing = 2.0**depth
        diagonal = diagonal_of(metrics[depth], spacing, pinned_levels[depth])
        for repeat in range(NU):
            values = sweep(depth, values, source, diagonal)
        applied = apply_local(values, metrics[depth], spacing, pinned_levels[depth])
        residual = source - applied
        coarse_source = restrict(residual)
        if depth == 1:
            correction, fine = coarse_correction(coarse_source, metric_two, gathered)
            applied = applied + stencil_apply(
                fine[1:], metrics[depth], fine[:-1, :, 1:-1], spacing, None
            )
            values = values + prolong(correction)
            values = values + OMEGA * (source - applied) / diagonal
            remaining = NU - 1
        else:
            correction = cycle(1, None, coarse_source)
            values = values + prolong(correction)
            remaining = NU
        for repeat in range(remaining):
            values = sweep(depth, values, source, diagonal)
        return values

    solution = None
    for repeat in range(CYCLES):
        solution = cycle(0, solution, right_side)
    return solution


def solution(mesh):
    placed = (
        P("tm", None, "space", None, None),
        P("tm", "space", None, None),
        P("space", None, None),
    )
    return jax.shard_map(
        per_device,
        mesh=mesh,
        in_specs=placed,
        out_specs=P("tm", None, "space", None, None),
        check_vma=False,
    )
```

```python
import functools

import jax
import jax.numpy as jnp
from jax import lax
from jax.experimental import pallas as pl
from jax.experimental.pallas import tpu as pltpu
from jax.sharding import PartitionSpec as P

CYCLES = 2
NU = 2
COARSE_SWEEPS = 4


OMEGA = 0.6


def with_halo(block, sides, width):
    for axis, dim in sides:
        count = lax.axis_size(axis)
        forward = [(i, i + 1) for i in range(count - 1)]
        backward = [(target, source) for source, target in forward]
        low = lax.ppermute(
            lax.slice_in_dim(block, block.shape[dim] - width, None, axis=dim), axis, forward
        )
        high = lax.ppermute(lax.slice_in_dim(block, 0, width, axis=dim), axis, backward)
        block = jnp.concatenate([low, block, high], axis=dim)
    return block


def from_behind(array, axis, by):
    size = lax.axis_size(axis)
    pairs = [(i, i + by) for i in range(size) if 0 <= i + by < size]
    return lax.ppermute(array, axis, pairs)


def stencil_apply(padded, metric, earlier, spacing, pinned):
    center = padded[:, :, 1:-1]
    ahead_x = padded[:, :, 2:]
    behind_x = padded[:, :, :-2]
    padded_yz = jnp.pad(center, ((0, 0), (0, 0), (0, 0), (1, 1), (1, 1)))
    ahead_y = padded_yz[:, :, :, 2:, 1:-1]
    behind_y = padded_yz[:, :, :, :-2, 1:-1]
    ahead_z = padded_yz[:, :, :, 1:-1, 2:]
    behind_z = padded_yz[:, :, :, 1:-1, :-2]
    inverse_square = 1.0 / (spacing * spacing)
    half_inverse = 0.5 / spacing
    laplace = (
        6.0 * center - ahead_x - behind_x - ahead_y - behind_y - ahead_z - behind_z
    ) * inverse_square
    grad_x = (ahead_x[:, 3] - behind_x[:, 3]) * half_inverse
    grad_y = (ahead_y[:, 3] - behind_y[:, 3]) * half_inverse
    grad_z = (ahead_z[:, 3] - behind_z[:, 3]) * half_inverse
    divergence = (
        ahead_x[:, 0]
        - behind_x[:, 0]
        + (ahead_y[:, 1] - behind_y[:, 1])
        + (ahead_z[:, 2] - behind_z[:, 2])
    ) * half_inverse
    coupling = jnp.stack([grad_x, grad_y, grad_z, divergence], axis=1)
    result = 2.0 * metric[:, None] * (center - earlier) + laplace + coupling
    if pinned is None:
        return result
    return jnp.where(pinned > 0, center, result)


def diagonal_of(metric, spacing, pinned):
    diagonal = 2.0 * metric[:, None] + 6.0 / (spacing * spacing)
    if pinned is None:
        return diagonal
    return jnp.where(pinned > 0, 1.0, diagonal)


def build_pinned(wall_mask):
    moving = (wall_mask > 0).astype(jnp.int32)
    walled = (wall_mask == 1).astype(jnp.int32)
    return jnp.stack([moving, walled, walled, jnp.zeros_like(walled)], axis=0)[None]


def pair_matrix(wide):
    fine = lax.broadcasted_iota(jnp.int32, (wide, wide // 2), 0)
    coarse = lax.broadcasted_iota(jnp.int32, (wide, wide // 2), 1)
    return (fine // 2 == coarse).astype(jnp.float32)


def restrict(values):
    summed = values[..., 0::2, :, :] + values[..., 1::2, :, :]
    summed = summed[..., 0::2, :] + summed[..., 1::2, :]
    summed = jnp.einsum(
        "...z,zw->...w", summed, pair_matrix(summed.shape[-1]), precision=lax.Precision.HIGHEST
    )
    return summed * 0.125


def prolong(values):
    spread = jnp.einsum(
        "...w,zw->...z",
        values,
        pair_matrix(2 * values.shape[-1]),
        precision=lax.Precision.HIGHEST,
    )
    spread = jnp.repeat(spread, 2, axis=-2)
    return jnp.repeat(spread, 2, axis=-3)


def coarse_kernel(src_ref, met_ref, out_ref, *, spacing, components, height_y, width_z):
    steps, rows, lanes = src_ref.shape
    depth_x = rows // components
    inverse_square = 1.0 / (spacing * spacing)
    half_inverse = 0.5 / spacing
    row = lax.broadcasted_iota(jnp.int32, (rows, lanes), 0)
    lane = lax.broadcasted_iota(jnp.int32, (rows, lanes), 1)
    plane = row // components
    part = row % components
    across_z = lane % width_z
    across_y = lane // width_z
    zero = jnp.zeros((rows, lanes), jnp.float32)

    def rolled(v, shift, axis):
        return pltpu.roll(v, shift % v.shape[axis], axis)

    def shifted(v, shift, axis, edge):
        return jnp.where(edge, zero, rolled(v, shift, axis))

    def apply(v, two_g):
        ahead_x = shifted(v, -components, 0, plane == depth_x - 1)
        behind_x = shifted(v, components, 0, plane == 0)
        ahead_y = shifted(v, -width_z, 1, across_y == height_y - 1)
        behind_y = shifted(v, width_z, 1, across_y == 0)
        ahead_z = shifted(v, -1, 1, across_z == width_z - 1)
        behind_z = shifted(v, 1, 1, across_z == 0)
        laplace = (6.0 * v - ahead_x - behind_x - ahead_y - behind_y - ahead_z - behind_z) * inverse_square
        diff_x = ahead_x - behind_x
        diff_y = ahead_y - behind_y
        diff_z = ahead_z - behind_z
        grad_x = rolled(diff_x, -3, 0)
        grad_y = rolled(diff_y, -2, 0)
        grad_z = rolled(diff_z, -1, 0)
        divergence = rolled(diff_x, 3, 0) + rolled(diff_y, 2, 0) + rolled(diff_z, 1, 0)
        coupling = jnp.where(part == 0, grad_x, jnp.where(part == 1, grad_y, jnp.where(part == 2, grad_z, divergence))) * half_inverse
        return two_g * v + laplace + coupling

    def advance(t, earlier):
        g = met_ref[t]
        two_g = 2.0 * g
        diagonal = two_g + 6.0 / (spacing * spacing)
        target = src_ref[t] + two_g * earlier
        v = target / diagonal
        for repeat in range(COARSE_SWEEPS - 1):
            v = v + (target - apply(v, two_g)) / diagonal
        out_ref[t] = v
        return v

    lax.fori_loop(0, steps, advance, zero)


def coarse_solve(flat_source, flat_metric, spacing, components, height_y, width_z):
    kernel = functools.partial(
        coarse_kernel, spacing=spacing, components=components, height_y=height_y, width_z=width_z
    )
    return pl.pallas_call(
        kernel,
        out_shape=jax.ShapeDtypeStruct(flat_source.shape, jnp.float32),
    )(flat_source, jnp.repeat(flat_metric, components, axis=1))


def apply_local(values, metric, spacing, pinned):
    padded = with_halo(values, (("space", 2),), 1)
    arrived = from_behind(values, "tm", 1)
    earlier = jnp.concatenate([arrived, values[:-1]], axis=0)
    return stencil_apply(padded, metric, earlier, spacing, pinned)


def assemble(flat_source, flat_metric, time_devs, plane_devs, local_dims):
    local_steps, components, planes, height_y, width_z = local_dims
    lanes = height_y * width_z
    whole_source = flat_source.reshape(
        time_devs, plane_devs, local_steps, components, planes, lanes
    )
    whole_source = whole_source.transpose(0, 2, 1, 4, 3, 5).reshape(
        time_devs * local_steps, plane_devs * planes * components, lanes
    )
    whole_metric = flat_metric.reshape(time_devs, plane_devs, local_steps, planes, lanes)
    whole_metric = whole_metric.transpose(0, 2, 1, 3, 4).reshape(
        time_devs * local_steps, plane_devs * planes, lanes
    )
    return (whole_source, whole_metric)


def gather_all(flat):
    across = lax.all_gather(flat, "tm", axis=0, tiled=True)
    whole = lax.all_gather(across, "space", axis=1, tiled=True)
    return whole.reshape(-1, flat.shape[1])


def coarse_correction(source, metric_two, gathered):
    time_devs = lax.axis_size("tm")
    plane_devs = lax.axis_size("space")
    time_at = lax.axis_index("tm")
    plane_at = lax.axis_index("space")
    local_dims = source.shape
    local_steps, components, planes, height_y, width_z = local_dims
    source_flat = source.reshape(1, -1)
    cut = source_flat.shape[1]
    if "metric" in gathered:
        flat_source = gather_all(source_flat)
        flat_metric = gathered["metric"]
    else:
        both = jnp.concatenate([source_flat, metric_two.reshape(1, -1)], axis=1)
        flat_both = gather_all(both)
        flat_source = flat_both[:, :cut]
        flat_metric = flat_both[:, cut:]
        gathered["metric"] = flat_metric
    whole_source, whole_metric = assemble(
        flat_source, flat_metric, time_devs, plane_devs, local_dims
    )
    solved = coarse_solve(whole_source, whole_metric, 4.0, components, height_y, width_z)
    mine = lax.dynamic_slice(
        solved,
        (time_at * local_steps, plane_at * planes * components, 0),
        (local_steps, planes * components, height_y * width_z),
    )
    mine = mine.reshape(local_steps, planes, components, height_y, width_z)
    padded = jnp.pad(solved, ((1, 0), (components, components), (0, 0)))
    around = lax.dynamic_slice(
        padded,
        (time_at * local_steps, plane_at * planes * components, 0),
        (local_steps + 1, (planes + 2) * components, height_y * width_z),
    )
    around = around.reshape(local_steps + 1, planes + 2, components, height_y, width_z)
    fine = prolong(around.transpose(0, 2, 1, 3, 4))[:, :, 1:-1]
    return (mine.transpose(0, 2, 1, 3, 4), fine)


def per_device(right_side, metric, wall_mask):
    pinned = build_pinned(wall_mask)
    metric_one = restrict(metric)
    metric_two = restrict(metric_one)
    metrics = (metric, metric_one)
    pinned_levels = (pinned, None)
    gathered = {}

    def sweep(depth, values, source, diagonal):
        if values is None:
            return OMEGA * source / diagonal
        spacing = 2.0**depth
        applied = apply_local(values, metrics[depth], spacing, pinned_levels[depth])
        return values + OMEGA * (source - applied) / diagonal

    def cycle(depth, values, source):
        spacing = 2.0**depth
        diagonal = diagonal_of(metrics[depth], spacing, pinned_levels[depth])
        for repeat in range(NU):
            values = sweep(depth, values, source, diagonal)
        applied = apply_local(values, metrics[depth], spacing, pinned_levels[depth])
        residual = source - applied
        coarse_source = restrict(residual)
        if depth == 1:
            correction, fine = coarse_correction(coarse_source, metric_two, gathered)
            applied = applied + stencil_apply(
                fine[1:], metrics[depth], fine[:-1, :, 1:-1], spacing, None
            )
            values = values + prolong(correction)
            values = values + OMEGA * (source - applied) / diagonal
            remaining = NU - 1
        else:
            correction = cycle(1, None, coarse_source)
            values = values + prolong(correction)
            remaining = NU
        for repeat in range(remaining):
            values = sweep(depth, values, source, diagonal)
        return values

    solution = None
    for repeat in range(CYCLES):
        solution = cycle(0, solution, right_side)
    return solution


def solution(mesh):
    placed = (
        P("tm", None, "space", None, None),
        P("tm", "space", None, None),
        P("space", None, None),
    )
    return jax.shard_map(
        per_device,
        mesh=mesh,
        in_specs=placed,
        out_specs=P("tm", None, "space", None, None),
        check_vma=False,
    )
```

```python
import functools

import jax
import jax.numpy as jnp
from jax import lax
from jax.experimental import pallas as pl
from jax.experimental.pallas import tpu as pltpu
from jax.sharding import PartitionSpec as P

CYCLES = 2
NU = 2
COARSE_SWEEPS = 4


OMEGA = 0.6


def with_halo(block, sides, width):
    for axis, dim in sides:
        count = lax.axis_size(axis)
        forward = [(i, i + 1) for i in range(count - 1)]
        backward = [(target, source) for source, target in forward]
        low = lax.ppermute(
            lax.slice_in_dim(block, block.shape[dim] - width, None, axis=dim), axis, forward
        )
        high = lax.ppermute(lax.slice_in_dim(block, 0, width, axis=dim), axis, backward)
        block = jnp.concatenate([low, block, high], axis=dim)
    return block


def from_behind(array, axis, by):
    size = lax.axis_size(axis)
    pairs = [(i, i + by) for i in range(size) if 0 <= i + by < size]
    return lax.ppermute(array, axis, pairs)


def stencil_apply(padded, metric, earlier, spacing, pinned):
    center = padded[:, :, 1:-1]
    ahead_x = padded[:, :, 2:]
    behind_x = padded[:, :, :-2]
    padded_yz = jnp.pad(center, ((0, 0), (0, 0), (0, 0), (1, 1), (1, 1)))
    ahead_y = padded_yz[:, :, :, 2:, 1:-1]
    behind_y = padded_yz[:, :, :, :-2, 1:-1]
    ahead_z = padded_yz[:, :, :, 1:-1, 2:]
    behind_z = padded_yz[:, :, :, 1:-1, :-2]
    inverse_square = 1.0 / (spacing * spacing)
    half_inverse = 0.5 / spacing
    laplace = (
        6.0 * center - ahead_x - behind_x - ahead_y - behind_y - ahead_z - behind_z
    ) * inverse_square
    grad_x = (ahead_x[:, 3] - behind_x[:, 3]) * half_inverse
    grad_y = (ahead_y[:, 3] - behind_y[:, 3]) * half_inverse
    grad_z = (ahead_z[:, 3] - behind_z[:, 3]) * half_inverse
    divergence = (
        ahead_x[:, 0]
        - behind_x[:, 0]
        + (ahead_y[:, 1] - behind_y[:, 1])
        + (ahead_z[:, 2] - behind_z[:, 2])
    ) * half_inverse
    coupling = jnp.stack([grad_x, grad_y, grad_z, divergence], axis=1)
    result = 2.0 * metric[:, None] * (center - earlier) + laplace + coupling
    if pinned is None:
        return result
    return jnp.where(pinned > 0, center, result)


def diagonal_of(metric, spacing, pinned):
    diagonal = 2.0 * metric[:, None] + 6.0 / (spacing * spacing)
    if pinned is None:
        return diagonal
    return jnp.where(pinned > 0, 1.0, diagonal)


def build_pinned(wall_mask):
    moving = (wall_mask > 0).astype(jnp.int32)
    walled = (wall_mask == 1).astype(jnp.int32)
    return jnp.stack([moving, walled, walled, jnp.zeros_like(walled)], axis=0)[None]


def pair_matrix(wide):
    fine = lax.broadcasted_iota(jnp.int32, (wide, wide // 2), 0)
    coarse = lax.broadcasted_iota(jnp.int32, (wide, wide // 2), 1)
    return (fine // 2 == coarse).astype(jnp.float32)


def restrict(values):
    summed = values[..., 0::2, :, :] + values[..., 1::2, :, :]
    summed = summed[..., 0::2, :] + summed[..., 1::2, :]
    summed = jnp.einsum(
        "...z,zw->...w", summed, pair_matrix(summed.shape[-1]), precision=lax.Precision.HIGHEST
    )
    return summed * 0.125


def prolong(values):
    spread = jnp.einsum(
        "...w,zw->...z",
        values,
        pair_matrix(2 * values.shape[-1]),
        precision=lax.Precision.HIGHEST,
    )
    spread = jnp.repeat(spread, 2, axis=-2)
    return jnp.repeat(spread, 2, axis=-3)


def coarse_kernel(src_ref, met_ref, out_ref, *, spacing, components, height_y, width_z):
    steps, rows, lanes = src_ref.shape
    depth_x = rows // components
    inverse_square = 1.0 / (spacing * spacing)
    half_inverse = 0.5 / spacing
    row = lax.broadcasted_iota(jnp.int32, (rows, lanes), 0)
    lane = lax.broadcasted_iota(jnp.int32, (rows, lanes), 1)
    plane = row // components
    part = row % components
    across_z = lane % width_z
    across_y = lane // width_z
    zero = jnp.zeros((rows, lanes), jnp.float32)

    def rolled(v, shift, axis):
        return pltpu.roll(v, shift % v.shape[axis], axis)

    def shifted(v, shift, axis, edge):
        return jnp.where(edge, zero, rolled(v, shift, axis))

    def apply(v, two_g):
        ahead_x = shifted(v, -components, 0, plane == depth_x - 1)
        behind_x = shifted(v, components, 0, plane == 0)
        ahead_y = shifted(v, -width_z, 1, across_y == height_y - 1)
        behind_y = shifted(v, width_z, 1, across_y == 0)
        ahead_z = shifted(v, -1, 1, across_z == width_z - 1)
        behind_z = shifted(v, 1, 1, across_z == 0)
        laplace = (6.0 * v - ahead_x - behind_x - ahead_y - behind_y - ahead_z - behind_z) * inverse_square
        diff_x = ahead_x - behind_x
        diff_y = ahead_y - behind_y
        diff_z = ahead_z - behind_z
        grad_x = rolled(diff_x, -3, 0)
        grad_y = rolled(diff_y, -2, 0)
        grad_z = rolled(diff_z, -1, 0)
        divergence = rolled(diff_x, 3, 0) + rolled(diff_y, 2, 0) + rolled(diff_z, 1, 0)
        coupling = jnp.where(part == 0, grad_x, jnp.where(part == 1, grad_y, jnp.where(part == 2, grad_z, divergence))) * half_inverse
        return two_g * v + laplace + coupling

    def advance(t, earlier):
        g = met_ref[t]
        two_g = 2.0 * g
        diagonal = two_g + 6.0 / (spacing * spacing)
        target = src_ref[t] + two_g * earlier
        v = target / diagonal
        for repeat in range(COARSE_SWEEPS - 1):
            v = v + (target - apply(v, two_g)) / diagonal
        out_ref[t] = v
        return v

    lax.fori_loop(0, steps, advance, zero)


def coarse_solve(flat_source, flat_metric, spacing, components, height_y, width_z):
    kernel = functools.partial(
        coarse_kernel, spacing=spacing, components=components, height_y=height_y, width_z=width_z
    )
    return pl.pallas_call(
        kernel,
        out_shape=jax.ShapeDtypeStruct(flat_source.shape, jnp.float32),
    )(flat_source, jnp.repeat(flat_metric, components, axis=1))


def apply_local(values, metric, spacing, pinned):
    padded = with_halo(values, (("space", 2),), 1)
    arrived = from_behind(values, "tm", 1)
    earlier = jnp.concatenate([arrived, values[:-1]], axis=0)
    return stencil_apply(padded, metric, earlier, spacing, pinned)


def assemble(flat_source, flat_metric, time_devs, plane_devs, local_dims):
    local_steps, components, planes, height_y, width_z = local_dims
    lanes = height_y * width_z
    whole_source = flat_source.reshape(
        time_devs, plane_devs, local_steps, components, planes, lanes
    )
    whole_source = whole_source.transpose(0, 2, 1, 4, 3, 5).reshape(
        time_devs * local_steps, plane_devs * planes * components, lanes
    )
    whole_metric = flat_metric.reshape(time_devs, plane_devs, local_steps, planes, lanes)
    whole_metric = whole_metric.transpose(0, 2, 1, 3, 4).reshape(
        time_devs * local_steps, plane_devs * planes, lanes
    )
    return (whole_source, whole_metric)


def gather_all(flat):
    across = lax.all_gather(flat, "tm", axis=0, tiled=True)
    whole = lax.all_gather(across, "space", axis=1, tiled=True)
    return whole.reshape(-1, flat.shape[1])


def coarse_correction(source, metric_two, gathered):
    time_devs = lax.axis_size("tm")
    plane_devs = lax.axis_size("space")
    time_at = lax.axis_index("tm")
    plane_at = lax.axis_index("space")
    local_dims = source.shape
    local_steps, components, planes, height_y, width_z = local_dims
    source_flat = source.reshape(1, -1)
    cut = source_flat.shape[1]
    if "metric" in gathered:
        flat_source = gather_all(source_flat)
        flat_metric = gathered["metric"]
    else:
        both = jnp.concatenate([source_flat, metric_two.reshape(1, -1)], axis=1)
        flat_both = gather_all(both)
        flat_source = flat_both[:, :cut]
        flat_metric = flat_both[:, cut:]
        gathered["metric"] = flat_metric
    whole_source, whole_metric = assemble(
        flat_source, flat_metric, time_devs, plane_devs, local_dims
    )
    solved = coarse_solve(whole_source, whole_metric, 4.0, components, height_y, width_z)
    mine = lax.dynamic_slice(
        solved,
        (time_at * local_steps, plane_at * planes * components, 0),
        (local_steps, planes * components, height_y * width_z),
    )
    mine = mine.reshape(local_steps, planes, components, height_y, width_z)
    padded = jnp.pad(solved, ((1, 0), (components, components), (0, 0)))
    around = lax.dynamic_slice(
        padded,
        (time_at * local_steps, plane_at * planes * components, 0),
        (local_steps + 1, (planes + 2) * components, height_y * width_z),
    )
    around = around.reshape(local_steps + 1, planes + 2, components, height_y, width_z)
    fine = prolong(around.transpose(0, 2, 1, 3, 4))[:, :, 1:-1]
    return (mine.transpose(0, 2, 1, 3, 4), fine)


def per_device(right_side, metric, wall_mask):
    pinned = build_pinned(wall_mask)
    metric_one = restrict(metric)
    metric_two = restrict(metric_one)
    metrics = (metric, metric_one)
    pinned_levels = (pinned, None)
    gathered = {}

    def sweep(depth, values, source, diagonal):
        if values is None:
            return OMEGA * source / diagonal
        spacing = 2.0**depth
        applied = apply_local(values, metrics[depth], spacing, pinned_levels[depth])
        return values + OMEGA * (source - applied) / diagonal

    def cycle(depth, values, source):
        spacing = 2.0**depth
        diagonal = diagonal_of(metrics[depth], spacing, pinned_levels[depth])
        for repeat in range(NU):
            values = sweep(depth, values, source, diagonal)
        applied = apply_local(values, metrics[depth], spacing, pinned_levels[depth])
        residual = source - applied
        coarse_source = restrict(residual)
        if depth == 1:
            correction, fine = coarse_correction(coarse_source, metric_two, gathered)
            applied = applied + stencil_apply(
                fine[1:], metrics[depth], fine[:-1, :, 1:-1], spacing, None
            )
            values = values + prolong(correction)
            values = values + OMEGA * (source - applied) / diagonal
            remaining = NU - 1
        else:
            correction = cycle(1, None, coarse_source)
            around = with_halo(correction, (("space", 2),), 1)
            earlier = prolong(from_behind(correction, "tm", 1))
            fine = prolong(around)[:, :, 1:-1]
            applied = applied + stencil_apply(
                fine, metrics[depth], earlier, spacing, pinned_levels[depth]
            )
            values = values + fine[:, :, 1:-1]
            values = values + OMEGA * (source - applied) / diagonal
            remaining = NU - 1
        for repeat in range(remaining):
            values = sweep(depth, values, source, diagonal)
        return values

    solution = None
    for repeat in range(CYCLES):
        solution = cycle(0, solution, right_side)
    return solution


def solution(mesh):
    placed = (
        P("tm", None, "space", None, None),
        P("tm", "space", None, None),
        P("space", None, None),
    )
    return jax.shard_map(
        per_device,
        mesh=mesh,
        in_specs=placed,
        out_specs=P("tm", None, "space", None, None),
        check_vma=False,
    )
```

```python
import functools

import jax
import jax.numpy as jnp
from jax import lax
from jax.experimental import pallas as pl
from jax.experimental.pallas import tpu as pltpu
from jax.sharding import PartitionSpec as P

CYCLES = 2
NU = 2
COARSE_SWEEPS = 4


OMEGA = 0.6


def with_halo(block, sides, width):
    for axis, dim in sides:
        count = lax.axis_size(axis)
        forward = [(i, i + 1) for i in range(count - 1)]
        backward = [(target, source) for source, target in forward]
        low = lax.ppermute(
            lax.slice_in_dim(block, block.shape[dim] - width, None, axis=dim), axis, forward
        )
        high = lax.ppermute(lax.slice_in_dim(block, 0, width, axis=dim), axis, backward)
        block = jnp.concatenate([low, block, high], axis=dim)
    return block


def from_behind(array, axis, by):
    size = lax.axis_size(axis)
    pairs = [(i, i + by) for i in range(size) if 0 <= i + by < size]
    return lax.ppermute(array, axis, pairs)


def stencil_apply(padded, metric, earlier, spacing, pinned):
    center = padded[:, :, 1:-1]
    ahead_x = padded[:, :, 2:]
    behind_x = padded[:, :, :-2]
    padded_yz = jnp.pad(center, ((0, 0), (0, 0), (0, 0), (1, 1), (1, 1)))
    ahead_y = padded_yz[:, :, :, 2:, 1:-1]
    behind_y = padded_yz[:, :, :, :-2, 1:-1]
    ahead_z = padded_yz[:, :, :, 1:-1, 2:]
    behind_z = padded_yz[:, :, :, 1:-1, :-2]
    inverse_square = 1.0 / (spacing * spacing)
    half_inverse = 0.5 / spacing
    laplace = (
        6.0 * center - ahead_x - behind_x - ahead_y - behind_y - ahead_z - behind_z
    ) * inverse_square
    grad_x = (ahead_x[:, 3] - behind_x[:, 3]) * half_inverse
    grad_y = (ahead_y[:, 3] - behind_y[:, 3]) * half_inverse
    grad_z = (ahead_z[:, 3] - behind_z[:, 3]) * half_inverse
    divergence = (
        ahead_x[:, 0]
        - behind_x[:, 0]
        + (ahead_y[:, 1] - behind_y[:, 1])
        + (ahead_z[:, 2] - behind_z[:, 2])
    ) * half_inverse
    coupling = jnp.stack([grad_x, grad_y, grad_z, divergence], axis=1)
    result = 2.0 * metric[:, None] * (center - earlier) + laplace + coupling
    if pinned is None:
        return result
    return jnp.where(pinned > 0, center, result)


def diagonal_of(metric, spacing, pinned):
    diagonal = 2.0 * metric[:, None] + 6.0 / (spacing * spacing)
    if pinned is None:
        return diagonal
    return jnp.where(pinned > 0, 1.0, diagonal)


def build_pinned(wall_mask):
    moving = (wall_mask > 0).astype(jnp.int32)
    walled = (wall_mask == 1).astype(jnp.int32)
    return jnp.stack([moving, walled, walled, jnp.zeros_like(walled)], axis=0)[None]


def pair_matrix(wide):
    fine = lax.broadcasted_iota(jnp.int32, (wide, wide // 2), 0)
    coarse = lax.broadcasted_iota(jnp.int32, (wide, wide // 2), 1)
    return (fine // 2 == coarse).astype(jnp.float32)


def restrict(values):
    summed = values[..., 0::2, :, :] + values[..., 1::2, :, :]
    summed = summed[..., 0::2, :] + summed[..., 1::2, :]
    summed = jnp.einsum(
        "...z,zw->...w", summed, pair_matrix(summed.shape[-1]), precision=lax.Precision.HIGHEST
    )
    return summed * 0.125


def prolong(values):
    spread = jnp.einsum(
        "...w,zw->...z",
        values,
        pair_matrix(2 * values.shape[-1]),
        precision=lax.Precision.HIGHEST,
    )
    spread = jnp.repeat(spread, 2, axis=-2)
    return jnp.repeat(spread, 2, axis=-3)


def coarse_kernel(src_ref, met_ref, out_ref, *, spacing, components, height_y, width_z):
    steps, rows, lanes = src_ref.shape
    depth_x = rows // components
    inverse_square = 1.0 / (spacing * spacing)
    half_inverse = 0.5 / spacing
    row = lax.broadcasted_iota(jnp.int32, (rows, lanes), 0)
    lane = lax.broadcasted_iota(jnp.int32, (rows, lanes), 1)
    plane = row // components
    part = row % components
    across_z = lane % width_z
    across_y = lane // width_z
    zero = jnp.zeros((rows, lanes), jnp.float32)

    def rolled(v, shift, axis):
        return pltpu.roll(v, shift % v.shape[axis], axis)

    def shifted(v, shift, axis, edge):
        return jnp.where(edge, zero, rolled(v, shift, axis))

    def apply(v, two_g):
        ahead_x = shifted(v, -components, 0, plane == depth_x - 1)
        behind_x = shifted(v, components, 0, plane == 0)
        ahead_y = shifted(v, -width_z, 1, across_y == height_y - 1)
        behind_y = shifted(v, width_z, 1, across_y == 0)
        ahead_z = shifted(v, -1, 1, across_z == width_z - 1)
        behind_z = shifted(v, 1, 1, across_z == 0)
        laplace = (6.0 * v - ahead_x - behind_x - ahead_y - behind_y - ahead_z - behind_z) * inverse_square
        diff_x = ahead_x - behind_x
        diff_y = ahead_y - behind_y
        diff_z = ahead_z - behind_z
        grad_x = rolled(diff_x, -3, 0)
        grad_y = rolled(diff_y, -2, 0)
        grad_z = rolled(diff_z, -1, 0)
        divergence = rolled(diff_x, 3, 0) + rolled(diff_y, 2, 0) + rolled(diff_z, 1, 0)
        coupling = jnp.where(part == 0, grad_x, jnp.where(part == 1, grad_y, jnp.where(part == 2, grad_z, divergence))) * half_inverse
        return two_g * v + laplace + coupling

    def advance(t, earlier):
        g = met_ref[t]
        two_g = 2.0 * g
        diagonal = two_g + 6.0 / (spacing * spacing)
        target = src_ref[t] + two_g * earlier
        v = target / diagonal
        for repeat in range(COARSE_SWEEPS - 1):
            v = v + (target - apply(v, two_g)) / diagonal
        out_ref[t] = v
        return v

    lax.fori_loop(0, steps, advance, zero)


def coarse_solve(flat_source, flat_metric, spacing, components, height_y, width_z):
    kernel = functools.partial(
        coarse_kernel, spacing=spacing, components=components, height_y=height_y, width_z=width_z
    )
    return pl.pallas_call(
        kernel,
        out_shape=jax.ShapeDtypeStruct(flat_source.shape, jnp.float32),
    )(flat_source, jnp.repeat(flat_metric, components, axis=1))


def earlier_of(values):
    arrived = from_behind(values[-1:], "tm", 1)
    return jnp.concatenate([arrived, values[:-1]], axis=0)


def apply_local(values, metric, spacing, pinned):
    padded = with_halo(values, (("space", 2),), 1)
    return stencil_apply(padded, metric, earlier_of(values), spacing, pinned)


def assemble(flat_source, flat_metric, time_devs, plane_devs, local_dims):
    local_steps, components, planes, height_y, width_z = local_dims
    lanes = height_y * width_z
    whole_source = flat_source.reshape(
        time_devs, plane_devs, local_steps, components, planes, lanes
    )
    whole_source = whole_source.transpose(0, 2, 1, 4, 3, 5).reshape(
        time_devs * local_steps, plane_devs * planes * components, lanes
    )
    whole_metric = flat_metric.reshape(time_devs, plane_devs, local_steps, planes, lanes)
    whole_metric = whole_metric.transpose(0, 2, 1, 3, 4).reshape(
        time_devs * local_steps, plane_devs * planes, lanes
    )
    return (whole_source, whole_metric)


def gather_all(flat):
    across = lax.all_gather(flat, "tm", axis=0, tiled=True)
    whole = lax.all_gather(across, "space", axis=1, tiled=True)
    return whole.reshape(-1, flat.shape[1])


def coarse_correction(source, metric_two, gathered):
    time_devs = lax.axis_size("tm")
    plane_devs = lax.axis_size("space")
    time_at = lax.axis_index("tm")
    plane_at = lax.axis_index("space")
    local_dims = source.shape
    local_steps, components, planes, height_y, width_z = local_dims
    source_flat = source.reshape(1, -1)
    cut = source_flat.shape[1]
    if "metric" in gathered:
        flat_source = gather_all(source_flat)
        flat_metric = gathered["metric"]
    else:
        both = jnp.concatenate([source_flat, metric_two.reshape(1, -1)], axis=1)
        flat_both = gather_all(both)
        flat_source = flat_both[:, :cut]
        flat_metric = flat_both[:, cut:]
        gathered["metric"] = flat_metric
    whole_source, whole_metric = assemble(
        flat_source, flat_metric, time_devs, plane_devs, local_dims
    )
    solved = coarse_solve(whole_source, whole_metric, 4.0, components, height_y, width_z)
    mine = lax.dynamic_slice(
        solved,
        (time_at * local_steps, plane_at * planes * components, 0),
        (local_steps, planes * components, height_y * width_z),
    )
    mine = mine.reshape(local_steps, planes, components, height_y, width_z)
    padded = jnp.pad(solved, ((1, 0), (components, components), (0, 0)))
    around = lax.dynamic_slice(
        padded,
        (time_at * local_steps, plane_at * planes * components, 0),
        (local_steps + 1, (planes + 2) * components, height_y * width_z),
    )
    around = around.reshape(local_steps + 1, planes + 2, components, height_y, width_z)
    fine = prolong(around.transpose(0, 2, 1, 3, 4))[:, :, 1:-1]
    return (mine.transpose(0, 2, 1, 3, 4), fine)


def per_device(right_side, metric, wall_mask):
    pinned = build_pinned(wall_mask)
    metric_one = restrict(metric)
    metric_two = restrict(metric_one)
    metrics = (metric, metric_one)
    pinned_levels = (pinned, None)
    gathered = {}

    def sweep(depth, values, source, diagonal):
        if values is None:
            return OMEGA * source / diagonal
        spacing = 2.0**depth
        applied = apply_local(values, metrics[depth], spacing, pinned_levels[depth])
        return values + OMEGA * (source - applied) / diagonal

    def smooth_from_zero(depth, source):
        spacing = 2.0**depth
        metric_wide = with_halo(metrics[depth], (("space", 1),), 2)
        source_wide = with_halo(source, (("space", 2),), 2)
        diagonal_wide = diagonal_of(metric_wide, spacing, None)
        first = OMEGA * source_wide / diagonal_wide
        inner = first[:, :, 1:-1]
        earlier = earlier_of(inner)
        applied = stencil_apply(first, metric_wide[:, 1:-1], earlier, spacing, None)
        second = inner + OMEGA * (source_wide[:, :, 1:-1] - applied) / diagonal_wide[:, :, 1:-1]
        planes = source.shape[2]
        inside = lax.axis_index("space") * planes - 1 + lax.broadcasted_iota(jnp.int32, (planes + 2,), 0)
        inside = jnp.logical_and(inside >= 0, inside < planes * lax.axis_size("space"))
        second = jnp.where(inside[None, None, :, None, None], second, 0.0)
        values = second[:, :, 1:-1]
        applied = stencil_apply(second, metrics[depth], earlier_of(values), spacing, None)
        return (values, applied)

    def cycle(depth, values, source):
        spacing = 2.0**depth
        diagonal = diagonal_of(metrics[depth], spacing, pinned_levels[depth])
        if values is None and depth == 1 and NU == 2:
            values, applied = smooth_from_zero(depth, source)
        else:
            for repeat in range(NU):
                values = sweep(depth, values, source, diagonal)
            applied = apply_local(values, metrics[depth], spacing, pinned_levels[depth])
        residual = source - applied
        coarse_source = restrict(residual)
        if depth == 1:
            correction, fine = coarse_correction(coarse_source, metric_two, gathered)
            applied = applied + stencil_apply(
                fine[1:], metrics[depth], fine[:-1, :, 1:-1], spacing, None
            )
            values = values + prolong(correction)
            values = values + OMEGA * (source - applied) / diagonal
            remaining = NU - 1
        else:
            correction = cycle(1, None, coarse_source)
            values = values + prolong(correction)
            remaining = NU
        for repeat in range(remaining):
            values = sweep(depth, values, source, diagonal)
        return values

    solution = None
    for repeat in range(CYCLES):
        solution = cycle(0, solution, right_side)
    return solution


def solution(mesh):
    placed = (
        P("tm", None, "space", None, None),
        P("tm", "space", None, None),
        P("space", None, None),
    )
    return jax.shard_map(
        per_device,
        mesh=mesh,
        in_specs=placed,
        out_specs=P("tm", None, "space", None, None),
        check_vma=False,
    )
```

```python
import functools

import jax
import jax.numpy as jnp
from jax import lax
from jax.experimental import pallas as pl
from jax.experimental.pallas import tpu as pltpu
from jax.sharding import PartitionSpec as P

CYCLES = 2
NU = 2
COARSE_SWEEPS = 4


OMEGA = 0.6


def with_halo(block, sides, width):
    for axis, dim in sides:
        count = lax.axis_size(axis)
        forward = [(i, i + 1) for i in range(count - 1)]
        backward = [(target, source) for source, target in forward]
        low = lax.ppermute(
            lax.slice_in_dim(block, block.shape[dim] - width, None, axis=dim), axis, forward
        )
        high = lax.ppermute(lax.slice_in_dim(block, 0, width, axis=dim), axis, backward)
        block = jnp.concatenate([low, block, high], axis=dim)
    return block


def from_behind(array, axis, by):
    size = lax.axis_size(axis)
    pairs = [(i, i + by) for i in range(size) if 0 <= i + by < size]
    return lax.ppermute(array, axis, pairs)


def stencil_apply(padded, metric, earlier, spacing, pinned):
    center = padded[:, :, 1:-1]
    ahead_x = padded[:, :, 2:]
    behind_x = padded[:, :, :-2]
    padded_yz = jnp.pad(center, ((0, 0), (0, 0), (0, 0), (1, 1), (1, 1)))
    ahead_y = padded_yz[:, :, :, 2:, 1:-1]
    behind_y = padded_yz[:, :, :, :-2, 1:-1]
    ahead_z = padded_yz[:, :, :, 1:-1, 2:]
    behind_z = padded_yz[:, :, :, 1:-1, :-2]
    inverse_square = 1.0 / (spacing * spacing)
    half_inverse = 0.5 / spacing
    laplace = (
        6.0 * center - ahead_x - behind_x - ahead_y - behind_y - ahead_z - behind_z
    ) * inverse_square
    grad_x = (ahead_x[:, 3] - behind_x[:, 3]) * half_inverse
    grad_y = (ahead_y[:, 3] - behind_y[:, 3]) * half_inverse
    grad_z = (ahead_z[:, 3] - behind_z[:, 3]) * half_inverse
    divergence = (
        ahead_x[:, 0]
        - behind_x[:, 0]
        + (ahead_y[:, 1] - behind_y[:, 1])
        + (ahead_z[:, 2] - behind_z[:, 2])
    ) * half_inverse
    coupling = jnp.stack([grad_x, grad_y, grad_z, divergence], axis=1)
    result = 2.0 * metric[:, None] * (center - earlier) + laplace + coupling
    if pinned is None:
        return result
    return jnp.where(pinned > 0, center, result)


def diagonal_of(metric, spacing, pinned):
    diagonal = 2.0 * metric[:, None] + 6.0 / (spacing * spacing)
    if pinned is None:
        return diagonal
    return jnp.where(pinned > 0, 1.0, diagonal)


def build_pinned(wall_mask):
    moving = (wall_mask > 0).astype(jnp.int32)
    walled = (wall_mask == 1).astype(jnp.int32)
    return jnp.stack([moving, walled, walled, jnp.zeros_like(walled)], axis=0)[None]


def pair_matrix(wide):
    fine = lax.broadcasted_iota(jnp.int32, (wide, wide // 2), 0)
    coarse = lax.broadcasted_iota(jnp.int32, (wide, wide // 2), 1)
    return (fine // 2 == coarse).astype(jnp.float32)


def restrict(values):
    summed = values[..., 0::2, :, :] + values[..., 1::2, :, :]
    summed = summed[..., 0::2, :] + summed[..., 1::2, :]
    summed = jnp.einsum(
        "...z,zw->...w", summed, pair_matrix(summed.shape[-1]), precision=lax.Precision.HIGHEST
    )
    return summed * 0.125


def prolong(values):
    spread = jnp.einsum(
        "...w,zw->...z",
        values,
        pair_matrix(2 * values.shape[-1]),
        precision=lax.Precision.HIGHEST,
    )
    spread = jnp.repeat(spread, 2, axis=-2)
    return jnp.repeat(spread, 2, axis=-3)


def coarse_kernel(src_ref, met_ref, out_ref, *, spacing, components, height_y, width_z):
    steps, rows, lanes = src_ref.shape
    depth_x = rows // components
    inverse_square = 1.0 / (spacing * spacing)
    half_inverse = 0.5 / spacing
    row = lax.broadcasted_iota(jnp.int32, (rows, lanes), 0)
    lane = lax.broadcasted_iota(jnp.int32, (rows, lanes), 1)
    plane = row // components
    part = row % components
    across_z = lane % width_z
    across_y = lane // width_z
    zero = jnp.zeros((rows, lanes), jnp.float32)

    def rolled(v, shift, axis):
        return pltpu.roll(v, shift % v.shape[axis], axis)

    def shifted(v, shift, axis, edge):
        return jnp.where(edge, zero, rolled(v, shift, axis))

    def apply(v, two_g):
        ahead_x = shifted(v, -components, 0, plane == depth_x - 1)
        behind_x = shifted(v, components, 0, plane == 0)
        ahead_y = shifted(v, -width_z, 1, across_y == height_y - 1)
        behind_y = shifted(v, width_z, 1, across_y == 0)
        ahead_z = shifted(v, -1, 1, across_z == width_z - 1)
        behind_z = shifted(v, 1, 1, across_z == 0)
        laplace = (6.0 * v - ahead_x - behind_x - ahead_y - behind_y - ahead_z - behind_z) * inverse_square
        diff_x = ahead_x - behind_x
        diff_y = ahead_y - behind_y
        diff_z = ahead_z - behind_z
        grad_x = rolled(diff_x, -3, 0)
        grad_y = rolled(diff_y, -2, 0)
        grad_z = rolled(diff_z, -1, 0)
        divergence = rolled(diff_x, 3, 0) + rolled(diff_y, 2, 0) + rolled(diff_z, 1, 0)
        coupling = jnp.where(part == 0, grad_x, jnp.where(part == 1, grad_y, jnp.where(part == 2, grad_z, divergence))) * half_inverse
        return two_g * v + laplace + coupling

    def advance(t, earlier):
        g = met_ref[t]
        two_g = 2.0 * g
        diagonal = two_g + 6.0 / (spacing * spacing)
        target = src_ref[t] + two_g * earlier
        v = target / diagonal
        for repeat in range(COARSE_SWEEPS - 1):
            v = v + (target - apply(v, two_g)) / diagonal
        out_ref[t] = v
        return v

    lax.fori_loop(0, steps, advance, zero)


def coarse_solve(flat_source, flat_metric, spacing, components, height_y, width_z):
    kernel = functools.partial(
        coarse_kernel, spacing=spacing, components=components, height_y=height_y, width_z=width_z
    )
    return pl.pallas_call(
        kernel,
        out_shape=jax.ShapeDtypeStruct(flat_source.shape, jnp.float32),
    )(flat_source, jnp.repeat(flat_metric, components, axis=1))


def apply_local(values, metric, spacing, pinned):
    padded = with_halo(values, (("space", 2),), 1)
    arrived = from_behind(values, "tm", 1)
    earlier = jnp.concatenate([arrived, values[:-1]], axis=0)
    return stencil_apply(padded, metric, earlier, spacing, pinned)


def assemble(flat_source, flat_metric, time_devs, plane_devs, local_dims):
    local_steps, components, planes, height_y, width_z = local_dims
    lanes = height_y * width_z
    whole_source = flat_source.reshape(
        time_devs, plane_devs, local_steps, components, planes, lanes
    )
    whole_source = whole_source.transpose(0, 2, 1, 4, 3, 5).reshape(
        time_devs * local_steps, plane_devs * planes * components, lanes
    )
    whole_metric = flat_metric.reshape(time_devs, plane_devs, local_steps, planes, lanes)
    whole_metric = whole_metric.transpose(0, 2, 1, 3, 4).reshape(
        time_devs * local_steps, plane_devs * planes, lanes
    )
    return (whole_source, whole_metric)


def gather_all(flat):
    across = lax.all_gather(flat, "tm", axis=0, tiled=True)
    whole = lax.all_gather(across.reshape(1, -1), "space", axis=0, tiled=True)
    whole = whole.reshape(lax.axis_size("space"), lax.axis_size("tm"), flat.shape[1])
    return whole.transpose(1, 0, 2).reshape(-1, flat.shape[1])


def coarse_correction(source, metric_two, gathered):
    time_devs = lax.axis_size("tm")
    plane_devs = lax.axis_size("space")
    time_at = lax.axis_index("tm")
    plane_at = lax.axis_index("space")
    local_dims = source.shape
    local_steps, components, planes, height_y, width_z = local_dims
    source_flat = source.reshape(1, -1)
    cut = source_flat.shape[1]
    if "metric" in gathered:
        flat_source = gather_all(source_flat)
        flat_metric = gathered["metric"]
    else:
        both = jnp.concatenate([source_flat, metric_two.reshape(1, -1)], axis=1)
        flat_both = gather_all(both)
        flat_source = flat_both[:, :cut]
        flat_metric = flat_both[:, cut:]
        gathered["metric"] = flat_metric
    whole_source, whole_metric = assemble(
        flat_source, flat_metric, time_devs, plane_devs, local_dims
    )
    solved = coarse_solve(whole_source, whole_metric, 4.0, components, height_y, width_z)
    mine = lax.dynamic_slice(
        solved,
        (time_at * local_steps, plane_at * planes * components, 0),
        (local_steps, planes * components, height_y * width_z),
    )
    mine = mine.reshape(local_steps, planes, components, height_y, width_z)
    padded = jnp.pad(solved, ((1, 0), (components, components), (0, 0)))
    around = lax.dynamic_slice(
        padded,
        (time_at * local_steps, plane_at * planes * components, 0),
        (local_steps + 1, (planes + 2) * components, height_y * width_z),
    )
    around = around.reshape(local_steps + 1, planes + 2, components, height_y, width_z)
    fine = prolong(around.transpose(0, 2, 1, 3, 4))[:, :, 1:-1]
    return (mine.transpose(0, 2, 1, 3, 4), fine)


def per_device(right_side, metric, wall_mask):
    pinned = build_pinned(wall_mask)
    metric_one = restrict(metric)
    metric_two = restrict(metric_one)
    metrics = (metric, metric_one)
    pinned_levels = (pinned, None)
    gathered = {}

    def sweep(depth, values, source, diagonal):
        if values is None:
            return OMEGA * source / diagonal
        spacing = 2.0**depth
        applied = apply_local(values, metrics[depth], spacing, pinned_levels[depth])
        return values + OMEGA * (source - applied) / diagonal

    def cycle(depth, values, source):
        spacing = 2.0**depth
        diagonal = diagonal_of(metrics[depth], spacing, pinned_levels[depth])
        for repeat in range(NU):
            values = sweep(depth, values, source, diagonal)
        applied = apply_local(values, metrics[depth], spacing, pinned_levels[depth])
        residual = source - applied
        coarse_source = restrict(residual)
        if depth == 1:
            correction, fine = coarse_correction(coarse_source, metric_two, gathered)
            applied = applied + stencil_apply(
                fine[1:], metrics[depth], fine[:-1, :, 1:-1], spacing, None
            )
            values = values + prolong(correction)
            values = values + OMEGA * (source - applied) / diagonal
            remaining = NU - 1
        else:
            correction = cycle(1, None, coarse_source)
            values = values + prolong(correction)
            remaining = NU
        for repeat in range(remaining):
            values = sweep(depth, values, source, diagonal)
        return values

    solution = None
    for repeat in range(CYCLES):
        solution = cycle(0, solution, right_side)
    return solution


def solution(mesh):
    placed = (
        P("tm", None, "space", None, None),
        P("tm", "space", None, None),
        P("space", None, None),
    )
    return jax.shard_map(
        per_device,
        mesh=mesh,
        in_specs=placed,
        out_specs=P("tm", None, "space", None, None),
        check_vma=False,
    )
```

```python
import functools

import jax
import jax.numpy as jnp
from jax import lax
from jax.experimental import pallas as pl
from jax.experimental.pallas import tpu as pltpu
from jax.sharding import PartitionSpec as P

CYCLES = 2
NU = 2
COARSE_SWEEPS = 4


OMEGA = 0.6


def with_halo(block, sides, width):
    for axis, dim in sides:
        count = lax.axis_size(axis)
        forward = [(i, i + 1) for i in range(count - 1)]
        backward = [(target, source) for source, target in forward]
        low = lax.ppermute(
            lax.slice_in_dim(block, block.shape[dim] - width, None, axis=dim), axis, forward
        )
        high = lax.ppermute(lax.slice_in_dim(block, 0, width, axis=dim), axis, backward)
        block = jnp.concatenate([low, block, high], axis=dim)
    return block


def from_behind(array, axis, by):
    size = lax.axis_size(axis)
    pairs = [(i, i + by) for i in range(size) if 0 <= i + by < size]
    return lax.ppermute(array, axis, pairs)


def stencil_apply(padded, metric, earlier, spacing, pinned):
    center = padded[:, :, 1:-1]
    ahead_x = padded[:, :, 2:]
    behind_x = padded[:, :, :-2]
    padded_yz = jnp.pad(center, ((0, 0), (0, 0), (0, 0), (1, 1), (1, 1)))
    ahead_y = padded_yz[:, :, :, 2:, 1:-1]
    behind_y = padded_yz[:, :, :, :-2, 1:-1]
    ahead_z = padded_yz[:, :, :, 1:-1, 2:]
    behind_z = padded_yz[:, :, :, 1:-1, :-2]
    inverse_square = 1.0 / (spacing * spacing)
    half_inverse = 0.5 / spacing
    laplace = (
        6.0 * center - ahead_x - behind_x - ahead_y - behind_y - ahead_z - behind_z
    ) * inverse_square
    grad_x = (ahead_x[:, 3] - behind_x[:, 3]) * half_inverse
    grad_y = (ahead_y[:, 3] - behind_y[:, 3]) * half_inverse
    grad_z = (ahead_z[:, 3] - behind_z[:, 3]) * half_inverse
    divergence = (
        ahead_x[:, 0]
        - behind_x[:, 0]
        + (ahead_y[:, 1] - behind_y[:, 1])
        + (ahead_z[:, 2] - behind_z[:, 2])
    ) * half_inverse
    coupling = jnp.stack([grad_x, grad_y, grad_z, divergence], axis=1)
    result = 2.0 * metric[:, None] * (center - earlier) + laplace + coupling
    if pinned is None:
        return result
    return jnp.where(pinned > 0, center, result)


def diagonal_of(metric, spacing, pinned):
    diagonal = 2.0 * metric[:, None] + 6.0 / (spacing * spacing)
    if pinned is None:
        return diagonal
    return jnp.where(pinned > 0, 1.0, diagonal)


def build_pinned(wall_mask):
    moving = (wall_mask > 0).astype(jnp.int32)
    walled = (wall_mask == 1).astype(jnp.int32)
    return jnp.stack([moving, walled, walled, jnp.zeros_like(walled)], axis=0)[None]


def pair_matrix(wide):
    fine = lax.broadcasted_iota(jnp.int32, (wide, wide // 2), 0)
    coarse = lax.broadcasted_iota(jnp.int32, (wide, wide // 2), 1)
    return (fine // 2 == coarse).astype(jnp.float32)


def restrict(values):
    summed = values[..., 0::2, :, :] + values[..., 1::2, :, :]
    summed = summed[..., 0::2, :] + summed[..., 1::2, :]
    summed = jnp.einsum(
        "...z,zw->...w", summed, pair_matrix(summed.shape[-1]), precision=lax.Precision.HIGHEST
    )
    return summed * 0.125


def prolong(values):
    spread = jnp.einsum(
        "...w,zw->...z",
        values,
        pair_matrix(2 * values.shape[-1]),
        precision=lax.Precision.HIGHEST,
    )
    spread = jnp.repeat(spread, 2, axis=-2)
    return jnp.repeat(spread, 2, axis=-3)


def coarse_kernel(src_ref, met_ref, out_ref, *, spacing, components, height_y, width_z):
    steps, rows, lanes = src_ref.shape
    depth_x = rows // components
    inverse_square = 1.0 / (spacing * spacing)
    half_inverse = 0.5 / spacing
    row = lax.broadcasted_iota(jnp.int32, (rows, lanes), 0)
    lane = lax.broadcasted_iota(jnp.int32, (rows, lanes), 1)
    plane = row // components
    part = row % components
    across_z = lane % width_z
    across_y = lane // width_z
    zero = jnp.zeros((rows, lanes), jnp.float32)

    def rolled(v, shift, axis):
        return pltpu.roll(v, shift % v.shape[axis], axis)

    def shifted(v, shift, axis, edge):
        return jnp.where(edge, zero, rolled(v, shift, axis))

    def apply(v, two_g):
        ahead_x = shifted(v, -components, 0, plane == depth_x - 1)
        behind_x = shifted(v, components, 0, plane == 0)
        ahead_y = shifted(v, -width_z, 1, across_y == height_y - 1)
        behind_y = shifted(v, width_z, 1, across_y == 0)
        ahead_z = shifted(v, -1, 1, across_z == width_z - 1)
        behind_z = shifted(v, 1, 1, across_z == 0)
        laplace = (6.0 * v - ahead_x - behind_x - ahead_y - behind_y - ahead_z - behind_z) * inverse_square
        diff_x = ahead_x - behind_x
        diff_y = ahead_y - behind_y
        diff_z = ahead_z - behind_z
        grad_x = rolled(diff_x, -3, 0)
        grad_y = rolled(diff_y, -2, 0)
        grad_z = rolled(diff_z, -1, 0)
        divergence = rolled(diff_x, 3, 0) + rolled(diff_y, 2, 0) + rolled(diff_z, 1, 0)
        coupling = jnp.where(part == 0, grad_x, jnp.where(part == 1, grad_y, jnp.where(part == 2, grad_z, divergence))) * half_inverse
        return two_g * v + laplace + coupling

    def advance(t, earlier):
        g = met_ref[t]
        two_g = 2.0 * g
        diagonal = two_g + 6.0 / (spacing * spacing)
        target = src_ref[t] + two_g * earlier
        v = target / diagonal
        for repeat in range(COARSE_SWEEPS - 1):
            v = v + (target - apply(v, two_g)) / diagonal
        out_ref[t] = v
        return v

    lax.fori_loop(0, steps, advance, zero)


def coarse_solve(flat_source, flat_metric, spacing, components, height_y, width_z):
    kernel = functools.partial(
        coarse_kernel, spacing=spacing, components=components, height_y=height_y, width_z=width_z
    )
    return pl.pallas_call(
        kernel,
        out_shape=jax.ShapeDtypeStruct(flat_source.shape, jnp.float32),
    )(flat_source, jnp.repeat(flat_metric, components, axis=1))


def apply_local(values, metric, spacing, pinned):
    padded = with_halo(values, (("space", 2),), 1)
    arrived = from_behind(values, "tm", 1)
    earlier = jnp.concatenate([arrived, values[:-1]], axis=0)
    return stencil_apply(padded, metric, earlier, spacing, pinned)


def assemble(flat_source, flat_metric, time_devs, plane_devs, local_dims):
    local_steps, components, planes, height_y, width_z = local_dims
    lanes = height_y * width_z
    whole_source = flat_source.reshape(
        time_devs, plane_devs, local_steps, components, planes, lanes
    )
    whole_source = whole_source.transpose(0, 2, 1, 4, 3, 5).reshape(
        time_devs * local_steps, plane_devs * planes * components, lanes
    )
    whole_metric = flat_metric.reshape(time_devs, plane_devs, local_steps, planes, lanes)
    whole_metric = whole_metric.transpose(0, 2, 1, 3, 4).reshape(
        time_devs * local_steps, plane_devs * planes, lanes
    )
    return (whole_source, whole_metric)


def gather_doubling(flat, axis):
    size = lax.axis_size(axis)
    position = lax.axis_index(axis)
    gathered = flat
    step = 1
    while step < size:
        other = lax.ppermute(gathered, axis, [(i, i ^ step) for i in range(size)])
        lower = (position & step) == 0
        gathered = jnp.where(
            lower,
            jnp.concatenate([gathered, other], axis=0),
            jnp.concatenate([other, gathered], axis=0),
        )
        step *= 2
    return gathered


def gather_all(flat):
    across = gather_doubling(flat, "tm")
    whole = lax.all_gather(across, "space", axis=1, tiled=True)
    return whole.reshape(-1, flat.shape[1])


def coarse_correction(source, metric_two, gathered):
    time_devs = lax.axis_size("tm")
    plane_devs = lax.axis_size("space")
    time_at = lax.axis_index("tm")
    plane_at = lax.axis_index("space")
    local_dims = source.shape
    local_steps, components, planes, height_y, width_z = local_dims
    source_flat = source.reshape(1, -1)
    cut = source_flat.shape[1]
    if "metric" in gathered:
        flat_source = gather_all(source_flat)
        flat_metric = gathered["metric"]
    else:
        both = jnp.concatenate([source_flat, metric_two.reshape(1, -1)], axis=1)
        flat_both = gather_all(both)
        flat_source = flat_both[:, :cut]
        flat_metric = flat_both[:, cut:]
        gathered["metric"] = flat_metric
    whole_source, whole_metric = assemble(
        flat_source, flat_metric, time_devs, plane_devs, local_dims
    )
    solved = coarse_solve(whole_source, whole_metric, 4.0, components, height_y, width_z)
    mine = lax.dynamic_slice(
        solved,
        (time_at * local_steps, plane_at * planes * components, 0),
        (local_steps, planes * components, height_y * width_z),
    )
    mine = mine.reshape(local_steps, planes, components, height_y, width_z)
    padded = jnp.pad(solved, ((1, 0), (components, components), (0, 0)))
    around = lax.dynamic_slice(
        padded,
        (time_at * local_steps, plane_at * planes * components, 0),
        (local_steps + 1, (planes + 2) * components, height_y * width_z),
    )
    around = around.reshape(local_steps + 1, planes + 2, components, height_y, width_z)
    fine = prolong(around.transpose(0, 2, 1, 3, 4))[:, :, 1:-1]
    return (mine.transpose(0, 2, 1, 3, 4), fine)


def per_device(right_side, metric, wall_mask):
    pinned = build_pinned(wall_mask)
    metric_one = restrict(metric)
    metric_two = restrict(metric_one)
    metrics = (metric, metric_one)
    pinned_levels = (pinned, None)
    gathered = {}

    def sweep(depth, values, source, diagonal):
        if values is None:
            return OMEGA * source / diagonal
        spacing = 2.0**depth
        applied = apply_local(values, metrics[depth], spacing, pinned_levels[depth])
        return values + OMEGA * (source - applied) / diagonal

    def cycle(depth, values, source):
        spacing = 2.0**depth
        diagonal = diagonal_of(metrics[depth], spacing, pinned_levels[depth])
        for repeat in range(NU):
            values = sweep(depth, values, source, diagonal)
        applied = apply_local(values, metrics[depth], spacing, pinned_levels[depth])
        residual = source - applied
        coarse_source = restrict(residual)
        if depth == 1:
            correction, fine = coarse_correction(coarse_source, metric_two, gathered)
            applied = applied + stencil_apply(
                fine[1:], metrics[depth], fine[:-1, :, 1:-1], spacing, None
            )
            values = values + prolong(correction)
            values = values + OMEGA * (source - applied) / diagonal
            remaining = NU - 1
        else:
            correction = cycle(1, None, coarse_source)
            values = values + prolong(correction)
            remaining = NU
        for repeat in range(remaining):
            values = sweep(depth, values, source, diagonal)
        return values

    solution = None
    for repeat in range(CYCLES):
        solution = cycle(0, solution, right_side)
    return solution


def solution(mesh):
    placed = (
        P("tm", None, "space", None, None),
        P("tm", "space", None, None),
        P("space", None, None),
    )
    return jax.shard_map(
        per_device,
        mesh=mesh,
        in_specs=placed,
        out_specs=P("tm", None, "space", None, None),
        check_vma=False,
    )
```

```python
import functools

import jax
import jax.numpy as jnp
from jax import lax
from jax.experimental import pallas as pl
from jax.experimental.pallas import tpu as pltpu
from jax.sharding import PartitionSpec as P

CYCLES = 2
NU = 2
COARSE_SWEEPS = 4


OMEGA = 0.6


def with_halo(block, sides, width):
    for axis, dim in sides:
        count = lax.axis_size(axis)
        forward = [(i, i + 1) for i in range(count - 1)]
        backward = [(target, source) for source, target in forward]
        low = lax.ppermute(
            lax.slice_in_dim(block, block.shape[dim] - width, None, axis=dim), axis, forward
        )
        high = lax.ppermute(lax.slice_in_dim(block, 0, width, axis=dim), axis, backward)
        block = jnp.concatenate([low, block, high], axis=dim)
    return block


def from_behind(array, axis, by):
    size = lax.axis_size(axis)
    pairs = [(i, i + by) for i in range(size) if 0 <= i + by < size]
    return lax.ppermute(array, axis, pairs)


def stencil_apply(padded, metric, earlier, spacing, pinned):
    center = padded[:, :, 1:-1]
    ahead_x = padded[:, :, 2:]
    behind_x = padded[:, :, :-2]
    padded_yz = jnp.pad(center, ((0, 0), (0, 0), (0, 0), (1, 1), (1, 1)))
    ahead_y = padded_yz[:, :, :, 2:, 1:-1]
    behind_y = padded_yz[:, :, :, :-2, 1:-1]
    ahead_z = padded_yz[:, :, :, 1:-1, 2:]
    behind_z = padded_yz[:, :, :, 1:-1, :-2]
    inverse_square = 1.0 / (spacing * spacing)
    half_inverse = 0.5 / spacing
    laplace = (
        6.0 * center - ahead_x - behind_x - ahead_y - behind_y - ahead_z - behind_z
    ) * inverse_square
    grad_x = (ahead_x[:, 3] - behind_x[:, 3]) * half_inverse
    grad_y = (ahead_y[:, 3] - behind_y[:, 3]) * half_inverse
    grad_z = (ahead_z[:, 3] - behind_z[:, 3]) * half_inverse
    divergence = (
        ahead_x[:, 0]
        - behind_x[:, 0]
        + (ahead_y[:, 1] - behind_y[:, 1])
        + (ahead_z[:, 2] - behind_z[:, 2])
    ) * half_inverse
    coupling = jnp.stack([grad_x, grad_y, grad_z, divergence], axis=1)
    result = 2.0 * metric[:, None] * (center - earlier) + laplace + coupling
    if pinned is None:
        return result
    return jnp.where(pinned > 0, center, result)


def diagonal_of(metric, spacing, pinned):
    diagonal = 2.0 * metric[:, None] + 6.0 / (spacing * spacing)
    if pinned is None:
        return diagonal
    return jnp.where(pinned > 0, 1.0, diagonal)


def build_pinned(wall_mask):
    moving = (wall_mask > 0).astype(jnp.int32)
    walled = (wall_mask == 1).astype(jnp.int32)
    return jnp.stack([moving, walled, walled, jnp.zeros_like(walled)], axis=0)[None]


def pair_matrix(wide):
    fine = lax.broadcasted_iota(jnp.int32, (wide, wide // 2), 0)
    coarse = lax.broadcasted_iota(jnp.int32, (wide, wide // 2), 1)
    return (fine // 2 == coarse).astype(jnp.float32)


def restrict(values):
    summed = values[..., 0::2, :, :] + values[..., 1::2, :, :]
    summed = summed[..., 0::2, :] + summed[..., 1::2, :]
    summed = jnp.einsum(
        "...z,zw->...w", summed, pair_matrix(summed.shape[-1]), precision=lax.Precision.HIGHEST
    )
    return summed * 0.125


def prolong(values):
    spread = jnp.einsum(
        "...w,zw->...z",
        values,
        pair_matrix(2 * values.shape[-1]),
        precision=lax.Precision.HIGHEST,
    )
    spread = jnp.repeat(spread, 2, axis=-2)
    return jnp.repeat(spread, 2, axis=-3)


def coarse_kernel(src_ref, met_ref, out_ref, *, spacing, components, height_y, width_z):
    steps, rows, lanes = src_ref.shape
    depth_x = rows // components
    inverse_square = 1.0 / (spacing * spacing)
    half_inverse = 0.5 / spacing
    row = lax.broadcasted_iota(jnp.int32, (rows, lanes), 0)
    lane = lax.broadcasted_iota(jnp.int32, (rows, lanes), 1)
    plane = row // components
    part = row % components
    across_z = lane % width_z
    across_y = lane // width_z
    zero = jnp.zeros((rows, lanes), jnp.float32)

    def rolled(v, shift, axis):
        return pltpu.roll(v, shift % v.shape[axis], axis)

    def shifted(v, shift, axis, edge):
        return jnp.where(edge, zero, rolled(v, shift, axis))

    def apply(v, two_g):
        ahead_x = shifted(v, -components, 0, plane == depth_x - 1)
        behind_x = shifted(v, components, 0, plane == 0)
        ahead_y = shifted(v, -width_z, 1, across_y == height_y - 1)
        behind_y = shifted(v, width_z, 1, across_y == 0)
        ahead_z = shifted(v, -1, 1, across_z == width_z - 1)
        behind_z = shifted(v, 1, 1, across_z == 0)
        laplace = (6.0 * v - ahead_x - behind_x - ahead_y - behind_y - ahead_z - behind_z) * inverse_square
        diff_x = ahead_x - behind_x
        diff_y = ahead_y - behind_y
        diff_z = ahead_z - behind_z
        grad_x = rolled(diff_x, -3, 0)
        grad_y = rolled(diff_y, -2, 0)
        grad_z = rolled(diff_z, -1, 0)
        divergence = rolled(diff_x, 3, 0) + rolled(diff_y, 2, 0) + rolled(diff_z, 1, 0)
        coupling = jnp.where(part == 0, grad_x, jnp.where(part == 1, grad_y, jnp.where(part == 2, grad_z, divergence))) * half_inverse
        return two_g * v + laplace + coupling

    def advance(t, earlier):
        g = met_ref[t]
        two_g = 2.0 * g
        diagonal = two_g + 6.0 / (spacing * spacing)
        target = src_ref[t] + two_g * earlier
        v = target / diagonal
        for repeat in range(COARSE_SWEEPS - 1):
            v = v + (target - apply(v, two_g)) / diagonal
        out_ref[t] = v
        return v

    lax.fori_loop(0, steps, advance, zero)


def coarse_solve(flat_source, flat_metric, spacing, components, height_y, width_z):
    kernel = functools.partial(
        coarse_kernel, spacing=spacing, components=components, height_y=height_y, width_z=width_z
    )
    return pl.pallas_call(
        kernel,
        out_shape=jax.ShapeDtypeStruct(flat_source.shape, jnp.float32),
    )(flat_source, jnp.repeat(flat_metric, components, axis=1))


def apply_local(values, metric, spacing, pinned):
    padded = with_halo(values, (("space", 2),), 1)
    arrived = from_behind(values, "tm", 1)
    earlier = jnp.concatenate([arrived, values[:-1]], axis=0)
    return stencil_apply(padded, metric, earlier, spacing, pinned)


def assemble(flat_source, flat_metric, time_devs, plane_devs, local_dims):
    local_steps, components, planes, height_y, width_z = local_dims
    lanes = height_y * width_z
    whole_source = flat_source.reshape(
        time_devs, plane_devs, local_steps, components, planes, lanes
    )
    whole_source = whole_source.transpose(0, 2, 1, 4, 3, 5).reshape(
        time_devs * local_steps, plane_devs * planes * components, lanes
    )
    whole_metric = flat_metric.reshape(time_devs, plane_devs, local_steps, planes, lanes)
    whole_metric = whole_metric.transpose(0, 2, 1, 3, 4).reshape(
        time_devs * local_steps, plane_devs * planes, lanes
    )
    return (whole_source, whole_metric)


def gather_doubling(flat, axis, dim):
    size = lax.axis_size(axis)
    position = lax.axis_index(axis)
    gathered = flat
    step = 1
    while step < size:
        other = lax.ppermute(gathered, axis, [(i, i ^ step) for i in range(size)])
        lower = (position & step) == 0
        gathered = jnp.where(
            lower,
            jnp.concatenate([gathered, other], axis=dim),
            jnp.concatenate([other, gathered], axis=dim),
        )
        step *= 2
    return gathered


def gather_all(flat):
    across = gather_doubling(flat, "tm", 0)
    whole = gather_doubling(across, "space", 1)
    return whole.reshape(-1, flat.shape[1])


def coarse_correction(source, metric_two, gathered):
    time_devs = lax.axis_size("tm")
    plane_devs = lax.axis_size("space")
    time_at = lax.axis_index("tm")
    plane_at = lax.axis_index("space")
    local_dims = source.shape
    local_steps, components, planes, height_y, width_z = local_dims
    source_flat = source.reshape(1, -1)
    cut = source_flat.shape[1]
    if "metric" in gathered:
        flat_source = gather_all(source_flat)
        flat_metric = gathered["metric"]
    else:
        both = jnp.concatenate([source_flat, metric_two.reshape(1, -1)], axis=1)
        flat_both = gather_all(both)
        flat_source = flat_both[:, :cut]
        flat_metric = flat_both[:, cut:]
        gathered["metric"] = flat_metric
    whole_source, whole_metric = assemble(
        flat_source, flat_metric, time_devs, plane_devs, local_dims
    )
    solved = coarse_solve(whole_source, whole_metric, 4.0, components, height_y, width_z)
    mine = lax.dynamic_slice(
        solved,
        (time_at * local_steps, plane_at * planes * components, 0),
        (local_steps, planes * components, height_y * width_z),
    )
    mine = mine.reshape(local_steps, planes, components, height_y, width_z)
    padded = jnp.pad(solved, ((1, 0), (components, components), (0, 0)))
    around = lax.dynamic_slice(
        padded,
        (time_at * local_steps, plane_at * planes * components, 0),
        (local_steps + 1, (planes + 2) * components, height_y * width_z),
    )
    around = around.reshape(local_steps + 1, planes + 2, components, height_y, width_z)
    fine = prolong(around.transpose(0, 2, 1, 3, 4))[:, :, 1:-1]
    return (mine.transpose(0, 2, 1, 3, 4), fine)


def per_device(right_side, metric, wall_mask):
    pinned = build_pinned(wall_mask)
    metric_one = restrict(metric)
    metric_two = restrict(metric_one)
    metrics = (metric, metric_one)
    pinned_levels = (pinned, None)
    gathered = {}

    def sweep(depth, values, source, diagonal):
        if values is None:
            return OMEGA * source / diagonal
        spacing = 2.0**depth
        applied = apply_local(values, metrics[depth], spacing, pinned_levels[depth])
        return values + OMEGA * (source - applied) / diagonal

    def cycle(depth, values, source):
        spacing = 2.0**depth
        diagonal = diagonal_of(metrics[depth], spacing, pinned_levels[depth])
        for repeat in range(NU):
            values = sweep(depth, values, source, diagonal)
        applied = apply_local(values, metrics[depth], spacing, pinned_levels[depth])
        residual = source - applied
        coarse_source = restrict(residual)
        if depth == 1:
            correction, fine = coarse_correction(coarse_source, metric_two, gathered)
            applied = applied + stencil_apply(
                fine[1:], metrics[depth], fine[:-1, :, 1:-1], spacing, None
            )
            values = values + prolong(correction)
            values = values + OMEGA * (source - applied) / diagonal
            remaining = NU - 1
        else:
            correction = cycle(1, None, coarse_source)
            values = values + prolong(correction)
            remaining = NU
        for repeat in range(remaining):
            values = sweep(depth, values, source, diagonal)
        return values

    solution = None
    for repeat in range(CYCLES):
        solution = cycle(0, solution, right_side)
    return solution


def solution(mesh):
    placed = (
        P("tm", None, "space", None, None),
        P("tm", "space", None, None),
        P("space", None, None),
    )
    return jax.shard_map(
        per_device,
        mesh=mesh,
        in_specs=placed,
        out_specs=P("tm", None, "space", None, None),
        check_vma=False,
    )
```

```python
import functools

import jax
import jax.numpy as jnp
from jax import lax
from jax.experimental import pallas as pl
from jax.experimental.pallas import tpu as pltpu
from jax.sharding import PartitionSpec as P

CYCLES = 2
NU = 2
COARSE_SWEEPS = 4


OMEGA = 0.6


def with_halo(block, sides, width):
    for axis, dim in sides:
        count = lax.axis_size(axis)
        forward = [(i, i + 1) for i in range(count - 1)]
        backward = [(target, source) for source, target in forward]
        low = lax.ppermute(
            lax.slice_in_dim(block, block.shape[dim] - width, None, axis=dim), axis, forward
        )
        high = lax.ppermute(lax.slice_in_dim(block, 0, width, axis=dim), axis, backward)
        block = jnp.concatenate([low, block, high], axis=dim)
    return block


def from_behind(array, axis, by):
    size = lax.axis_size(axis)
    pairs = [(i, i + by) for i in range(size) if 0 <= i + by < size]
    return lax.ppermute(array, axis, pairs)


def stencil_apply(padded, metric, earlier, spacing, pinned):
    center = padded[:, :, 1:-1]
    ahead_x = padded[:, :, 2:]
    behind_x = padded[:, :, :-2]
    padded_yz = jnp.pad(center, ((0, 0), (0, 0), (0, 0), (1, 1), (1, 1)))
    ahead_y = padded_yz[:, :, :, 2:, 1:-1]
    behind_y = padded_yz[:, :, :, :-2, 1:-1]
    ahead_z = padded_yz[:, :, :, 1:-1, 2:]
    behind_z = padded_yz[:, :, :, 1:-1, :-2]
    inverse_square = 1.0 / (spacing * spacing)
    half_inverse = 0.5 / spacing
    laplace = (
        6.0 * center - ahead_x - behind_x - ahead_y - behind_y - ahead_z - behind_z
    ) * inverse_square
    grad_x = (ahead_x[:, 3] - behind_x[:, 3]) * half_inverse
    grad_y = (ahead_y[:, 3] - behind_y[:, 3]) * half_inverse
    grad_z = (ahead_z[:, 3] - behind_z[:, 3]) * half_inverse
    divergence = (
        ahead_x[:, 0]
        - behind_x[:, 0]
        + (ahead_y[:, 1] - behind_y[:, 1])
        + (ahead_z[:, 2] - behind_z[:, 2])
    ) * half_inverse
    coupling = jnp.stack([grad_x, grad_y, grad_z, divergence], axis=1)
    result = 2.0 * metric[:, None] * (center - earlier) + laplace + coupling
    if pinned is None:
        return result
    return jnp.where(pinned > 0, center, result)


def diagonal_of(metric, spacing, pinned):
    diagonal = 2.0 * metric[:, None] + 6.0 / (spacing * spacing)
    if pinned is None:
        return diagonal
    return jnp.where(pinned > 0, 1.0, diagonal)


def build_pinned(wall_mask):
    moving = (wall_mask > 0).astype(jnp.int32)
    walled = (wall_mask == 1).astype(jnp.int32)
    return jnp.stack([moving, walled, walled, jnp.zeros_like(walled)], axis=0)[None]


def pair_matrix(wide):
    fine = lax.broadcasted_iota(jnp.int32, (wide, wide // 2), 0)
    coarse = lax.broadcasted_iota(jnp.int32, (wide, wide // 2), 1)
    return (fine // 2 == coarse).astype(jnp.float32)


def restrict(values):
    summed = values[..., 0::2, :, :] + values[..., 1::2, :, :]
    summed = summed[..., 0::2, :] + summed[..., 1::2, :]
    summed = jnp.einsum(
        "...z,zw->...w", summed, pair_matrix(summed.shape[-1]), precision=lax.Precision.HIGHEST
    )
    return summed * 0.125


def prolong(values):
    spread = jnp.einsum(
        "...w,zw->...z",
        values,
        pair_matrix(2 * values.shape[-1]),
        precision=lax.Precision.HIGHEST,
    )
    spread = jnp.repeat(spread, 2, axis=-2)
    return jnp.repeat(spread, 2, axis=-3)


def coarse_kernel(src_ref, met_ref, out_ref, *, spacing, components, height_y, width_z):
    steps, rows, lanes = src_ref.shape
    depth_x = rows // components
    inverse_square = 1.0 / (spacing * spacing)
    half_inverse = 0.5 / spacing
    row = lax.broadcasted_iota(jnp.int32, (rows, lanes), 0)
    lane = lax.broadcasted_iota(jnp.int32, (rows, lanes), 1)
    plane = row // components
    part = row % components
    across_z = lane % width_z
    across_y = lane // width_z
    zero = jnp.zeros((rows, lanes), jnp.float32)

    def rolled(v, shift, axis):
        return pltpu.roll(v, shift % v.shape[axis], axis)

    def shifted(v, shift, axis, edge):
        return jnp.where(edge, zero, rolled(v, shift, axis))

    def apply(v, two_g):
        ahead_x = shifted(v, -components, 0, plane == depth_x - 1)
        behind_x = shifted(v, components, 0, plane == 0)
        ahead_y = shifted(v, -width_z, 1, across_y == height_y - 1)
        behind_y = shifted(v, width_z, 1, across_y == 0)
        ahead_z = shifted(v, -1, 1, across_z == width_z - 1)
        behind_z = shifted(v, 1, 1, across_z == 0)
        laplace = (6.0 * v - ahead_x - behind_x - ahead_y - behind_y - ahead_z - behind_z) * inverse_square
        diff_x = ahead_x - behind_x
        diff_y = ahead_y - behind_y
        diff_z = ahead_z - behind_z
        grad_x = rolled(diff_x, -3, 0)
        grad_y = rolled(diff_y, -2, 0)
        grad_z = rolled(diff_z, -1, 0)
        divergence = rolled(diff_x, 3, 0) + rolled(diff_y, 2, 0) + rolled(diff_z, 1, 0)
        coupling = jnp.where(part == 0, grad_x, jnp.where(part == 1, grad_y, jnp.where(part == 2, grad_z, divergence))) * half_inverse
        return two_g * v + laplace + coupling

    def advance(t, earlier):
        g = met_ref[t]
        two_g = 2.0 * g
        diagonal = two_g + 6.0 / (spacing * spacing)
        target = src_ref[t] + two_g * earlier
        v = target / diagonal
        for repeat in range(COARSE_SWEEPS - 1):
            v = v + (target - apply(v, two_g)) / diagonal
        out_ref[t] = v
        return v

    lax.fori_loop(0, steps, advance, zero)


def coarse_solve(flat_source, flat_metric, spacing, components, height_y, width_z):
    kernel = functools.partial(
        coarse_kernel, spacing=spacing, components=components, height_y=height_y, width_z=width_z
    )
    return pl.pallas_call(
        kernel,
        out_shape=jax.ShapeDtypeStruct(flat_source.shape, jnp.float32),
    )(flat_source, jnp.repeat(flat_metric, components, axis=1))


def apply_local(values, metric, spacing, pinned):
    padded = with_halo(values, (("space", 2),), 1)
    arrived = from_behind(values, "tm", 1)
    earlier = jnp.concatenate([arrived, values[:-1]], axis=0)
    return stencil_apply(padded, metric, earlier, spacing, pinned)


def assemble(flat_source, flat_metric, time_devs, plane_devs, local_dims):
    local_steps, components, planes, height_y, width_z = local_dims
    lanes = height_y * width_z
    whole_source = flat_source.reshape(
        time_devs, plane_devs, local_steps, components, planes, lanes
    )
    whole_source = whole_source.transpose(0, 2, 1, 4, 3, 5).reshape(
        time_devs * local_steps, plane_devs * planes * components, lanes
    )
    whole_metric = flat_metric.reshape(time_devs, plane_devs, local_steps, planes, lanes)
    whole_metric = whole_metric.transpose(0, 2, 1, 3, 4).reshape(
        time_devs * local_steps, plane_devs * planes, lanes
    )
    return (whole_source, whole_metric)


def gather_doubling(flat, axis, dim):
    size = lax.axis_size(axis)
    position = lax.axis_index(axis)
    gathered = flat
    step = 1
    while step < size:
        other = lax.ppermute(gathered, axis, [(i, i ^ step) for i in range(size)])
        lower = (position & step) == 0
        gathered = jnp.where(
            lower,
            jnp.concatenate([gathered, other], axis=dim),
            jnp.concatenate([other, gathered], axis=dim),
        )
        step *= 2
    return gathered


def gather_all(flat):
    across = gather_doubling(flat, "space", 1)
    whole = gather_doubling(across, "tm", 0)
    return whole.reshape(-1, flat.shape[1])


def coarse_correction(source, metric_two, gathered):
    time_devs = lax.axis_size("tm")
    plane_devs = lax.axis_size("space")
    time_at = lax.axis_index("tm")
    plane_at = lax.axis_index("space")
    local_dims = source.shape
    local_steps, components, planes, height_y, width_z = local_dims
    source_flat = source.reshape(1, -1)
    cut = source_flat.shape[1]
    if "metric" in gathered:
        flat_source = gather_all(source_flat)
        flat_metric = gathered["metric"]
    else:
        both = jnp.concatenate([source_flat, metric_two.reshape(1, -1)], axis=1)
        flat_both = gather_all(both)
        flat_source = flat_both[:, :cut]
        flat_metric = flat_both[:, cut:]
        gathered["metric"] = flat_metric
    whole_source, whole_metric = assemble(
        flat_source, flat_metric, time_devs, plane_devs, local_dims
    )
    solved = coarse_solve(whole_source, whole_metric, 4.0, components, height_y, width_z)
    mine = lax.dynamic_slice(
        solved,
        (time_at * local_steps, plane_at * planes * components, 0),
        (local_steps, planes * components, height_y * width_z),
    )
    mine = mine.reshape(local_steps, planes, components, height_y, width_z)
    padded = jnp.pad(solved, ((1, 0), (components, components), (0, 0)))
    around = lax.dynamic_slice(
        padded,
        (time_at * local_steps, plane_at * planes * components, 0),
        (local_steps + 1, (planes + 2) * components, height_y * width_z),
    )
    around = around.reshape(local_steps + 1, planes + 2, components, height_y, width_z)
    fine = prolong(around.transpose(0, 2, 1, 3, 4))[:, :, 1:-1]
    return (mine.transpose(0, 2, 1, 3, 4), fine)


def per_device(right_side, metric, wall_mask):
    pinned = build_pinned(wall_mask)
    metric_one = restrict(metric)
    metric_two = restrict(metric_one)
    metrics = (metric, metric_one)
    pinned_levels = (pinned, None)
    gathered = {}

    def sweep(depth, values, source, diagonal):
        if values is None:
            return OMEGA * source / diagonal
        spacing = 2.0**depth
        applied = apply_local(values, metrics[depth], spacing, pinned_levels[depth])
        return values + OMEGA * (source - applied) / diagonal

    def cycle(depth, values, source):
        spacing = 2.0**depth
        diagonal = diagonal_of(metrics[depth], spacing, pinned_levels[depth])
        for repeat in range(NU):
            values = sweep(depth, values, source, diagonal)
        applied = apply_local(values, metrics[depth], spacing, pinned_levels[depth])
        residual = source - applied
        coarse_source = restrict(residual)
        if depth == 1:
            correction, fine = coarse_correction(coarse_source, metric_two, gathered)
            applied = applied + stencil_apply(
                fine[1:], metrics[depth], fine[:-1, :, 1:-1], spacing, None
            )
            values = values + prolong(correction)
            values = values + OMEGA * (source - applied) / diagonal
            remaining = NU - 1
        else:
            correction = cycle(1, None, coarse_source)
            values = values + prolong(correction)
            remaining = NU
        for repeat in range(remaining):
            values = sweep(depth, values, source, diagonal)
        return values

    solution = None
    for repeat in range(CYCLES):
        solution = cycle(0, solution, right_side)
    return solution


def solution(mesh):
    placed = (
        P("tm", None, "space", None, None),
        P("tm", "space", None, None),
        P("space", None, None),
    )
    return jax.shard_map(
        per_device,
        mesh=mesh,
        in_specs=placed,
        out_specs=P("tm", None, "space", None, None),
        check_vma=False,
    )
```

```python
import functools

import jax
import jax.numpy as jnp
from jax import lax
from jax.experimental import pallas as pl
from jax.experimental.pallas import tpu as pltpu
from jax.sharding import PartitionSpec as P

CYCLES = 2
NU = 2
COARSE_SWEEPS = 4


OMEGA = 0.6


def with_halo(block, sides, width):
    for axis, dim in sides:
        count = lax.axis_size(axis)
        forward = [(i, i + 1) for i in range(count - 1)]
        backward = [(target, source) for source, target in forward]
        low = lax.ppermute(
            lax.slice_in_dim(block, block.shape[dim] - width, None, axis=dim), axis, forward
        )
        high = lax.ppermute(lax.slice_in_dim(block, 0, width, axis=dim), axis, backward)
        block = jnp.concatenate([low, block, high], axis=dim)
    return block


def from_behind(array, axis, by):
    size = lax.axis_size(axis)
    pairs = [(i, i + by) for i in range(size) if 0 <= i + by < size]
    return lax.ppermute(array, axis, pairs)


def stencil_apply(padded, metric, earlier, spacing, pinned):
    center = padded[:, :, 1:-1]
    ahead_x = padded[:, :, 2:]
    behind_x = padded[:, :, :-2]
    padded_yz = jnp.pad(center, ((0, 0), (0, 0), (0, 0), (1, 1), (1, 1)))
    ahead_y = padded_yz[:, :, :, 2:, 1:-1]
    behind_y = padded_yz[:, :, :, :-2, 1:-1]
    ahead_z = padded_yz[:, :, :, 1:-1, 2:]
    behind_z = padded_yz[:, :, :, 1:-1, :-2]
    inverse_square = 1.0 / (spacing * spacing)
    half_inverse = 0.5 / spacing
    laplace = (
        6.0 * center - ahead_x - behind_x - ahead_y - behind_y - ahead_z - behind_z
    ) * inverse_square
    grad_x = (ahead_x[:, 3] - behind_x[:, 3]) * half_inverse
    grad_y = (ahead_y[:, 3] - behind_y[:, 3]) * half_inverse
    grad_z = (ahead_z[:, 3] - behind_z[:, 3]) * half_inverse
    divergence = (
        ahead_x[:, 0]
        - behind_x[:, 0]
        + (ahead_y[:, 1] - behind_y[:, 1])
        + (ahead_z[:, 2] - behind_z[:, 2])
    ) * half_inverse
    coupling = jnp.stack([grad_x, grad_y, grad_z, divergence], axis=1)
    result = 2.0 * metric[:, None] * (center - earlier) + laplace + coupling
    if pinned is None:
        return result
    return jnp.where(pinned > 0, center, result)


def diagonal_of(metric, spacing, pinned):
    diagonal = 2.0 * metric[:, None] + 6.0 / (spacing * spacing)
    if pinned is None:
        return diagonal
    return jnp.where(pinned > 0, 1.0, diagonal)


def build_pinned(wall_mask):
    moving = (wall_mask > 0).astype(jnp.int32)
    walled = (wall_mask == 1).astype(jnp.int32)
    return jnp.stack([moving, walled, walled, jnp.zeros_like(walled)], axis=0)[None]


def pair_matrix(wide):
    fine = lax.broadcasted_iota(jnp.int32, (wide, wide // 2), 0)
    coarse = lax.broadcasted_iota(jnp.int32, (wide, wide // 2), 1)
    return (fine // 2 == coarse).astype(jnp.float32)


def restrict(values):
    summed = values[..., 0::2, :, :] + values[..., 1::2, :, :]
    summed = summed[..., 0::2, :] + summed[..., 1::2, :]
    summed = jnp.einsum(
        "...z,zw->...w", summed, pair_matrix(summed.shape[-1]), precision=lax.Precision.HIGHEST
    )
    return summed * 0.125


def prolong(values):
    spread = jnp.einsum(
        "...w,zw->...z",
        values,
        pair_matrix(2 * values.shape[-1]),
        precision=lax.Precision.HIGHEST,
    )
    spread = jnp.repeat(spread, 2, axis=-2)
    return jnp.repeat(spread, 2, axis=-3)


def coarse_kernel(src_ref, met_ref, out_ref, *, spacing, components, height_y, width_z):
    steps, rows, lanes = src_ref.shape
    depth_x = rows // components
    inverse_square = 1.0 / (spacing * spacing)
    half_inverse = 0.5 / spacing
    row = lax.broadcasted_iota(jnp.int32, (rows, lanes), 0)
    lane = lax.broadcasted_iota(jnp.int32, (rows, lanes), 1)
    plane = row // components
    part = row % components
    across_z = lane % width_z
    across_y = lane // width_z
    zero = jnp.zeros((rows, lanes), jnp.float32)

    def rolled(v, shift, axis):
        return pltpu.roll(v, shift % v.shape[axis], axis)

    def shifted(v, shift, axis, edge):
        return jnp.where(edge, zero, rolled(v, shift, axis))

    def apply(v, two_g):
        ahead_x = shifted(v, -components, 0, plane == depth_x - 1)
        behind_x = shifted(v, components, 0, plane == 0)
        ahead_y = shifted(v, -width_z, 1, across_y == height_y - 1)
        behind_y = shifted(v, width_z, 1, across_y == 0)
        ahead_z = shifted(v, -1, 1, across_z == width_z - 1)
        behind_z = shifted(v, 1, 1, across_z == 0)
        laplace = (6.0 * v - ahead_x - behind_x - ahead_y - behind_y - ahead_z - behind_z) * inverse_square
        diff_x = ahead_x - behind_x
        diff_y = ahead_y - behind_y
        diff_z = ahead_z - behind_z
        grad_x = rolled(diff_x, -3, 0)
        grad_y = rolled(diff_y, -2, 0)
        grad_z = rolled(diff_z, -1, 0)
        divergence = rolled(diff_x, 3, 0) + rolled(diff_y, 2, 0) + rolled(diff_z, 1, 0)
        coupling = jnp.where(part == 0, grad_x, jnp.where(part == 1, grad_y, jnp.where(part == 2, grad_z, divergence))) * half_inverse
        return two_g * v + laplace + coupling

    def advance(t, earlier):
        g = met_ref[t]
        two_g = 2.0 * g
        diagonal = two_g + 6.0 / (spacing * spacing)
        target = src_ref[t] + two_g * earlier
        v = target / diagonal
        for repeat in range(COARSE_SWEEPS - 1):
            v = v + (target - apply(v, two_g)) / diagonal
        out_ref[t] = v
        return v

    lax.fori_loop(0, steps, advance, zero)


def coarse_solve(flat_source, flat_metric, spacing, components, height_y, width_z):
    kernel = functools.partial(
        coarse_kernel, spacing=spacing, components=components, height_y=height_y, width_z=width_z
    )
    return pl.pallas_call(
        kernel,
        out_shape=jax.ShapeDtypeStruct(flat_source.shape, jnp.float32),
    )(flat_source, jnp.repeat(flat_metric, components, axis=1))


def apply_local(values, metric, spacing, pinned):
    padded = with_halo(values, (("space", 2),), 1)
    arrived = from_behind(values, "tm", 1)
    earlier = jnp.concatenate([arrived, values[:-1]], axis=0)
    return stencil_apply(padded, metric, earlier, spacing, pinned)


def assemble(flat_source, flat_metric, time_devs, plane_devs, local_dims):
    local_steps, components, planes, height_y, width_z = local_dims
    lanes = height_y * width_z
    whole_source = flat_source.reshape(
        time_devs, plane_devs, local_steps, components, planes, lanes
    )
    whole_source = whole_source.transpose(0, 2, 1, 4, 3, 5).reshape(
        time_devs * local_steps, plane_devs * planes * components, lanes
    )
    whole_metric = flat_metric.reshape(time_devs, plane_devs, local_steps, planes, lanes)
    whole_metric = whole_metric.transpose(0, 2, 1, 3, 4).reshape(
        time_devs * local_steps, plane_devs * planes, lanes
    )
    return (whole_source, whole_metric)


def gather_doubling(flat, axis, dim):
    size = lax.axis_size(axis)
    position = lax.axis_index(axis)
    gathered = flat
    step = 1
    while step < size:
        other = lax.ppermute(gathered, axis, [(i, i ^ step) for i in range(size)])
        lower = (position & step) == 0
        gathered = jnp.where(
            lower,
            jnp.concatenate([gathered, other], axis=dim),
            jnp.concatenate([other, gathered], axis=dim),
        )
        step *= 2
    return gathered


def gather_all(flat):
    across = gather_doubling(flat, "space", 1)
    whole = gather_doubling(across, "tm", 0)
    return whole.reshape(-1, flat.shape[1])


def coarse_correction(source, metric_two, gathered):
    time_devs = lax.axis_size("tm")
    plane_devs = lax.axis_size("space")
    time_at = lax.axis_index("tm")
    plane_at = lax.axis_index("space")
    local_dims = source.shape
    local_steps, components, planes, height_y, width_z = local_dims
    source_flat = source.reshape(1, -1)
    flat_source = gather_all(source_flat)
    flat_metric = gathered["metric"]
    whole_source, whole_metric = assemble(
        flat_source, flat_metric, time_devs, plane_devs, local_dims
    )
    solved = coarse_solve(whole_source, whole_metric, 4.0, components, height_y, width_z)
    mine = lax.dynamic_slice(
        solved,
        (time_at * local_steps, plane_at * planes * components, 0),
        (local_steps, planes * components, height_y * width_z),
    )
    mine = mine.reshape(local_steps, planes, components, height_y, width_z)
    padded = jnp.pad(solved, ((1, 0), (components, components), (0, 0)))
    around = lax.dynamic_slice(
        padded,
        (time_at * local_steps, plane_at * planes * components, 0),
        (local_steps + 1, (planes + 2) * components, height_y * width_z),
    )
    around = around.reshape(local_steps + 1, planes + 2, components, height_y, width_z)
    fine = prolong(around.transpose(0, 2, 1, 3, 4))[:, :, 1:-1]
    return (mine.transpose(0, 2, 1, 3, 4), fine)


def per_device(right_side, metric, wall_mask):
    pinned = build_pinned(wall_mask)
    metric_one = restrict(metric)
    metric_two = restrict(metric_one)
    metrics = (metric, metric_one)
    pinned_levels = (pinned, None)
    gathered = {"metric": gather_all(metric_two.reshape(1, -1))}

    def sweep(depth, values, source, diagonal):
        if values is None:
            return OMEGA * source / diagonal
        spacing = 2.0**depth
        applied = apply_local(values, metrics[depth], spacing, pinned_levels[depth])
        return values + OMEGA * (source - applied) / diagonal

    def cycle(depth, values, source):
        spacing = 2.0**depth
        diagonal = diagonal_of(metrics[depth], spacing, pinned_levels[depth])
        for repeat in range(NU):
            values = sweep(depth, values, source, diagonal)
        applied = apply_local(values, metrics[depth], spacing, pinned_levels[depth])
        residual = source - applied
        coarse_source = restrict(residual)
        if depth == 1:
            correction, fine = coarse_correction(coarse_source, metric_two, gathered)
            applied = applied + stencil_apply(
                fine[1:], metrics[depth], fine[:-1, :, 1:-1], spacing, None
            )
            values = values + prolong(correction)
            values = values + OMEGA * (source - applied) / diagonal
            remaining = NU - 1
        else:
            correction = cycle(1, None, coarse_source)
            values = values + prolong(correction)
            remaining = NU
        for repeat in range(remaining):
            values = sweep(depth, values, source, diagonal)
        return values

    solution = None
    for repeat in range(CYCLES):
        solution = cycle(0, solution, right_side)
    return solution


def solution(mesh):
    placed = (
        P("tm", None, "space", None, None),
        P("tm", "space", None, None),
        P("space", None, None),
    )
    return jax.shard_map(
        per_device,
        mesh=mesh,
        in_specs=placed,
        out_specs=P("tm", None, "space", None, None),
        check_vma=False,
    )
```

```python
import functools

import jax
import jax.numpy as jnp
from jax import lax
from jax.experimental import pallas as pl
from jax.experimental.pallas import tpu as pltpu
from jax.sharding import PartitionSpec as P

CYCLES = 2
NU = 2
COARSE_SWEEPS = 4


OMEGA = 0.6


def with_halo(block, sides, width):
    for axis, dim in sides:
        count = lax.axis_size(axis)
        forward = [(i, i + 1) for i in range(count - 1)]
        backward = [(target, source) for source, target in forward]
        low = lax.ppermute(
            lax.slice_in_dim(block, block.shape[dim] - width, None, axis=dim), axis, forward
        )
        high = lax.ppermute(lax.slice_in_dim(block, 0, width, axis=dim), axis, backward)
        block = jnp.concatenate([low, block, high], axis=dim)
    return block


def from_behind(array, axis, by):
    size = lax.axis_size(axis)
    pairs = [(i, i + by) for i in range(size) if 0 <= i + by < size]
    return lax.ppermute(array, axis, pairs)


def stencil_apply(padded, metric, earlier, spacing, pinned):
    center = padded[:, :, 1:-1]
    ahead_x = padded[:, :, 2:]
    behind_x = padded[:, :, :-2]
    padded_yz = jnp.pad(center, ((0, 0), (0, 0), (0, 0), (1, 1), (1, 1)))
    ahead_y = padded_yz[:, :, :, 2:, 1:-1]
    behind_y = padded_yz[:, :, :, :-2, 1:-1]
    ahead_z = padded_yz[:, :, :, 1:-1, 2:]
    behind_z = padded_yz[:, :, :, 1:-1, :-2]
    inverse_square = 1.0 / (spacing * spacing)
    half_inverse = 0.5 / spacing
    laplace = (
        6.0 * center - ahead_x - behind_x - ahead_y - behind_y - ahead_z - behind_z
    ) * inverse_square
    grad_x = (ahead_x[:, 3] - behind_x[:, 3]) * half_inverse
    grad_y = (ahead_y[:, 3] - behind_y[:, 3]) * half_inverse
    grad_z = (ahead_z[:, 3] - behind_z[:, 3]) * half_inverse
    divergence = (
        ahead_x[:, 0]
        - behind_x[:, 0]
        + (ahead_y[:, 1] - behind_y[:, 1])
        + (ahead_z[:, 2] - behind_z[:, 2])
    ) * half_inverse
    coupling = jnp.stack([grad_x, grad_y, grad_z, divergence], axis=1)
    result = 2.0 * metric[:, None] * (center - earlier) + laplace + coupling
    if pinned is None:
        return result
    return jnp.where(pinned > 0, center, result)


def diagonal_of(metric, spacing, pinned):
    diagonal = 2.0 * metric[:, None] + 6.0 / (spacing * spacing)
    if pinned is None:
        return diagonal
    return jnp.where(pinned > 0, 1.0, diagonal)


def build_pinned(wall_mask):
    moving = (wall_mask > 0).astype(jnp.int32)
    walled = (wall_mask == 1).astype(jnp.int32)
    return jnp.stack([moving, walled, walled, jnp.zeros_like(walled)], axis=0)[None]


def pair_matrix(wide):
    fine = lax.broadcasted_iota(jnp.int32, (wide, wide // 2), 0)
    coarse = lax.broadcasted_iota(jnp.int32, (wide, wide // 2), 1)
    return (fine // 2 == coarse).astype(jnp.float32)


def restrict(values):
    summed = values[..., 0::2, :, :] + values[..., 1::2, :, :]
    summed = summed[..., 0::2, :] + summed[..., 1::2, :]
    summed = jnp.einsum(
        "...z,zw->...w", summed, pair_matrix(summed.shape[-1]), precision=lax.Precision.HIGHEST
    )
    return summed * 0.125


def prolong(values):
    spread = jnp.einsum(
        "...w,zw->...z",
        values,
        pair_matrix(2 * values.shape[-1]),
        precision=lax.Precision.HIGHEST,
    )
    spread = jnp.repeat(spread, 2, axis=-2)
    return jnp.repeat(spread, 2, axis=-3)


def coarse_kernel(src_ref, met_ref, out_ref, *, spacing, components, height_y, width_z):
    steps, rows, lanes = src_ref.shape
    depth_x = rows // components
    inverse_square = 1.0 / (spacing * spacing)
    half_inverse = 0.5 / spacing
    row = lax.broadcasted_iota(jnp.int32, (rows, lanes), 0)
    lane = lax.broadcasted_iota(jnp.int32, (rows, lanes), 1)
    plane = row // components
    part = row % components
    across_z = lane % width_z
    across_y = lane // width_z
    zero = jnp.zeros((rows, lanes), jnp.float32)

    def rolled(v, shift, axis):
        return pltpu.roll(v, shift % v.shape[axis], axis)

    def shifted(v, shift, axis, edge):
        return jnp.where(edge, zero, rolled(v, shift, axis))

    def apply(v, two_g):
        ahead_x = shifted(v, -components, 0, plane == depth_x - 1)
        behind_x = shifted(v, components, 0, plane == 0)
        ahead_y = shifted(v, -width_z, 1, across_y == height_y - 1)
        behind_y = shifted(v, width_z, 1, across_y == 0)
        ahead_z = shifted(v, -1, 1, across_z == width_z - 1)
        behind_z = shifted(v, 1, 1, across_z == 0)
        laplace = (6.0 * v - ahead_x - behind_x - ahead_y - behind_y - ahead_z - behind_z) * inverse_square
        diff_x = ahead_x - behind_x
        diff_y = ahead_y - behind_y
        diff_z = ahead_z - behind_z
        grad_x = rolled(diff_x, -3, 0)
        grad_y = rolled(diff_y, -2, 0)
        grad_z = rolled(diff_z, -1, 0)
        divergence = rolled(diff_x, 3, 0) + rolled(diff_y, 2, 0) + rolled(diff_z, 1, 0)
        coupling = jnp.where(part == 0, grad_x, jnp.where(part == 1, grad_y, jnp.where(part == 2, grad_z, divergence))) * half_inverse
        return two_g * v + laplace + coupling

    def advance(t, earlier):
        g = met_ref[t]
        two_g = 2.0 * g
        diagonal = two_g + 6.0 / (spacing * spacing)
        target = src_ref[t] + two_g * earlier
        v = target / diagonal
        for repeat in range(COARSE_SWEEPS - 1):
            v = v + (target - apply(v, two_g)) / diagonal
        out_ref[t] = v
        return v

    lax.fori_loop(0, steps, advance, zero)


def coarse_solve(flat_source, flat_metric, spacing, components, height_y, width_z):
    kernel = functools.partial(
        coarse_kernel, spacing=spacing, components=components, height_y=height_y, width_z=width_z
    )
    return pl.pallas_call(
        kernel,
        out_shape=jax.ShapeDtypeStruct(flat_source.shape, jnp.float32),
    )(flat_source, jnp.repeat(flat_metric, components, axis=1))


def apply_local(values, metric, spacing, pinned):
    padded = with_halo(values, (("space", 2),), 1)
    arrived = from_behind(values, "tm", 1)
    earlier = jnp.concatenate([arrived, values[:-1]], axis=0)
    return stencil_apply(padded, metric, earlier, spacing, pinned)


def assemble(flat_source, flat_metric, time_devs, plane_devs, local_dims):
    local_steps, components, planes, height_y, width_z = local_dims
    lanes = height_y * width_z
    whole_source = flat_source.reshape(
        time_devs, plane_devs, local_steps, components, planes, lanes
    )
    whole_source = whole_source.transpose(0, 2, 1, 4, 3, 5).reshape(
        time_devs * local_steps, plane_devs * planes * components, lanes
    )
    whole_metric = flat_metric.reshape(time_devs, plane_devs, local_steps, planes, lanes)
    whole_metric = whole_metric.transpose(0, 2, 1, 3, 4).reshape(
        time_devs * local_steps, plane_devs * planes, lanes
    )
    return (whole_source, whole_metric)


def gather_doubling(flat, axis, dim, widest_first=False):
    size = lax.axis_size(axis)
    position = lax.axis_index(axis)
    steps = []
    step = 1
    while step < size:
        steps.append(step)
        step *= 2
    if widest_first:
        steps = steps[::-1]
    gathered = flat
    for step in steps:
        other = lax.ppermute(gathered, axis, [(i, i ^ step) for i in range(size)])
        lower = (position & step) == 0
        gathered = jnp.where(
            lower,
            jnp.concatenate([gathered, other], axis=dim),
            jnp.concatenate([other, gathered], axis=dim),
        )
    if widest_first:
        count = len(steps)
        shape = gathered.shape
        split = shape[:dim] + (2,) * count + (shape[dim] // size,) + shape[dim + 1 :]
        order = (
            list(range(dim))
            + list(range(dim + count - 1, dim - 1, -1))
            + list(range(dim + count, len(split)))
        )
        gathered = gathered.reshape(split).transpose(order).reshape(shape)
    return gathered


def gather_all(flat):
    across = gather_doubling(flat, "space", 1)
    whole = gather_doubling(across, "tm", 0, widest_first=True)
    return whole.reshape(-1, flat.shape[1])


def coarse_correction(source, metric_two, gathered):
    time_devs = lax.axis_size("tm")
    plane_devs = lax.axis_size("space")
    time_at = lax.axis_index("tm")
    plane_at = lax.axis_index("space")
    local_dims = source.shape
    local_steps, components, planes, height_y, width_z = local_dims
    source_flat = source.reshape(1, -1)
    flat_source = gather_all(source_flat)
    flat_metric = gathered["metric"]
    whole_source, whole_metric = assemble(
        flat_source, flat_metric, time_devs, plane_devs, local_dims
    )
    solved = coarse_solve(whole_source, whole_metric, 4.0, components, height_y, width_z)
    mine = lax.dynamic_slice(
        solved,
        (time_at * local_steps, plane_at * planes * components, 0),
        (local_steps, planes * components, height_y * width_z),
    )
    mine = mine.reshape(local_steps, planes, components, height_y, width_z)
    padded = jnp.pad(solved, ((1, 0), (components, components), (0, 0)))
    around = lax.dynamic_slice(
        padded,
        (time_at * local_steps, plane_at * planes * components, 0),
        (local_steps + 1, (planes + 2) * components, height_y * width_z),
    )
    around = around.reshape(local_steps + 1, planes + 2, components, height_y, width_z)
    fine = prolong(around.transpose(0, 2, 1, 3, 4))[:, :, 1:-1]
    return (mine.transpose(0, 2, 1, 3, 4), fine)


def per_device(right_side, metric, wall_mask):
    pinned = build_pinned(wall_mask)
    metric_one = restrict(metric)
    metric_two = restrict(metric_one)
    metrics = (metric, metric_one)
    pinned_levels = (pinned, None)
    gathered = {"metric": gather_all(metric_two.reshape(1, -1))}

    def sweep(depth, values, source, diagonal):
        if values is None:
            return OMEGA * source / diagonal
        spacing = 2.0**depth
        applied = apply_local(values, metrics[depth], spacing, pinned_levels[depth])
        return values + OMEGA * (source - applied) / diagonal

    def cycle(depth, values, source):
        spacing = 2.0**depth
        diagonal = diagonal_of(metrics[depth], spacing, pinned_levels[depth])
        for repeat in range(NU):
            values = sweep(depth, values, source, diagonal)
        applied = apply_local(values, metrics[depth], spacing, pinned_levels[depth])
        residual = source - applied
        coarse_source = restrict(residual)
        if depth == 1:
            correction, fine = coarse_correction(coarse_source, metric_two, gathered)
            applied = applied + stencil_apply(
                fine[1:], metrics[depth], fine[:-1, :, 1:-1], spacing, None
            )
            values = values + prolong(correction)
            values = values + OMEGA * (source - applied) / diagonal
            remaining = NU - 1
        else:
            correction = cycle(1, None, coarse_source)
            values = values + prolong(correction)
            remaining = NU
        for repeat in range(remaining):
            values = sweep(depth, values, source, diagonal)
        return values

    solution = None
    for repeat in range(CYCLES):
        solution = cycle(0, solution, right_side)
    return solution


def solution(mesh):
    placed = (
        P("tm", None, "space", None, None),
        P("tm", "space", None, None),
        P("space", None, None),
    )
    return jax.shard_map(
        per_device,
        mesh=mesh,
        in_specs=placed,
        out_specs=P("tm", None, "space", None, None),
        check_vma=False,
    )
```
